128 devices in a mesh: ty: 16 (over x, z), tx: 8 (over y, core).
Axes of the slice: x: 4, y: 4, z: 4, core: 2. Of those that a mesh axis runs over, the one named last changes fastest.
Arguments:
- screen: float32 [1024, 2048], P('ty', 'tx'), may hold values from -6 to 6
- wind_table: float32 [2, 16], replicated, may hold values from -0.4 to 0.4
- wind_index: int32 [16, 8], P('ty', 'tx'), may hold values from 0 to 15
- tile_id: int32 [16, 8, 8, 32, 1], P('ty', 'tx'), may hold values from 0 to 127; in each aligned block of 256 rows (0 to 255, 256 to 511, ..., all dimensions but the last counted through in order) at most 4 rows name the same one
- cell_index: int32 [16, 8, 8, 32], P('ty', 'tx'), may hold values from 0 to 8000
- fractions: float32 [2, 16, 8, 8, 32], P(None, 'ty', 'tx'), may hold values from 0 to 1
Outputs:
- screen_next: float32 [1024, 2048], P('ty', 'tx')
- phases: float32 [16, 8, 8, 32, 128], P('ty', 'tx')
- slopes: float32 [16, 8, 8, 32, 128], P('ty', 'tx')
The draws below stay inside these ranges and needn't reach their ends.
Inputs may be any that keep to these rules, and one draw needn't show every extreme that they name: `tile_id`: among the 256 records of one station group and direction group, at most 4 name the same tile, a bound that some block reaches of them.
All inputs are finite; a program needn't handle non-finite values.
Results may differ from the reference program's by a relative error of at most 0.0003.
Values sent between devices are 32-bit elements; how exact they have to be, the bound alone decides.
No kernel may reach another device: no remote copies, remote signals or barrier semaphores. Data moves between devices by JAX's collectives and lax.ppermute only.
A program may use at most 64 MiB of HBM per device.

```python
import math
import jax
import jax.numpy as jnp
import numpy as np
from jax import lax

RY = 64
RX = 256
P_SIZE = 128
SD = 8
DD = 32
SUB = 4
NWIND = 16
NY = 1024
NX = 2048
CAP = 4
N_TY = 16
N_TX = 8


def place_ends(array, rng, smallest, largest):
    place = [jax.random.randint(jax.random.fold_in(rng, axis), (), 0, length) for axis, length in enumerate(array.shape)]
    main_axis = array.shape.index(max(array.shape))
    neighbour = place[:main_axis] + [(place[main_axis] + 1) % array.shape[main_axis]] + place[main_axis + 1:]
    return array.at[tuple(place)].set(smallest).at[tuple(neighbour)].set(largest)


def level_of(key, shape, pieces, least, top_value):
    level = 1.0
    for position, blocks in pieces:
        heights = jax.random.uniform(jax.random.fold_in(jax.random.fold_in(key, 6), position), (blocks,), jnp.float32, least / len(pieces), top_value / len(pieces))
        level = level * jnp.repeat(jnp.exp(heights), shape[position] // blocks).reshape((-1,) + (1,) * (len(shape) - 1 - position))
    return level


def deal_out(own_key, own, number, rows, amount, top, limit, slope):
    order = jax.random.permutation(own_key, amount)
    heavy_load, usual = portions_of(amount, rows * top, limit, slope, True), portions_of(amount, rows * top, limit, slope, False)
    places = jnp.arange(amount)

    def named(tallies, offset_by):
        used = int((tallies > 0).sum())
        fixed = max(1, used // 4)
        moved = fixed + (places - fixed + offset_by * (used - fixed)) % max(1, amount - fixed)
        return jnp.zeros((amount,), jnp.int32).at[order[jnp.where(places < fixed, places, moved)]].set(jnp.asarray(tallies, jnp.int32))

    tallies = jnp.where(number % 4 == 0, named(heavy_load, number // 4), named(usual, number - number // 4 - 1))
    mixed = jax.random.permutation(jax.random.fold_in(own, 3), amount)
    source_of, receiver = mixed[0:amount // 2 * 2:2], mixed[1:amount // 2 * 2:2]
    slack = jnp.minimum(tallies[source_of] - 1, limit - tallies[receiver]) // 2
    slack = jnp.where((source_of == order[0]) | (receiver == order[0]) | (tallies[receiver] == 0), 0, jnp.maximum(slack, 0))
    moved = jax.random.randint(jax.random.fold_in(own, 4), (amount // 2,), 0, 1 << 20) % (slack + 1)
    tallies = tallies.at[source_of].add(-moved).at[receiver].add(moved)
    members = jnp.searchsorted(jnp.cumsum(tallies), jnp.arange(rows * top), side="right").astype(jnp.int32)
    grid = members.reshape(top, rows).T
    grid = grid[jax.random.permutation(jax.random.fold_in(own, 1), rows)]
    offset_by = jax.random.randint(jax.random.fold_in(own, 2), (rows, 1), 0, top)
    return jnp.take_along_axis(grid, (jnp.arange(top)[None, :] + offset_by) % top, axis=1)


def portions_of(number_of, total, most, skew, full):
    weights = [(1 << 20) // math.isqrt(grade ** skew) + 1 for grade in range(1, number_of + 1)]
    largest = most if full else min(most, max(-(-total // number_of), total * weights[0] // sum(weights)))
    least = 1 if total - largest >= number_of - 1 else 0
    given, rest = [largest] + [least] * (number_of - 1), total - largest - least * (number_of - 1)
    while rest > 0:
        free = [i for i in range(1, number_of) if given[i] < largest] or [i for i in range(1, number_of) if given[i] < most]
        mass, budget = sum([weights[i] for i in free]), rest
        for i in free:
            more = min(most - given[i], max(1, budget * weights[i] // mass), rest)
            given[i] = given[i] + more
            rest = rest - more
    return np.array(given)


def noise(own_key, dims, deviation, most, shards=(), dtype=jnp.bfloat16):
    level = level_of(own_key, dims, shards, -0.22, 0.18) if shards else 1.0
    drawn = jax.random.normal(own_key, dims, jnp.float32) * deviation * level
    return jnp.minimum(jnp.maximum(drawn, -most), most).astype(dtype)


def setup_inputs(seed: int = 0) -> dict:
    key_of = jax.random.split(jax.random.key(seed), 7)
    screen = noise(key_of[0], (NY, NX), 1.0, 6.0, ((0, 16), (1, 8)), jnp.float32)
    wind_table = jnp.clip(jax.random.uniform(key_of[1], (2, NWIND), jnp.float32, -0.4, 0.4), -0.4, 0.4)
    wind_index = place_ends(jax.random.randint(key_of[2], (N_TY, N_TX), 0, NWIND), jax.random.fold_in(key_of[2], 1), 0, NWIND - 1).astype(jnp.int32)
    tile_id_keys = jax.random.split(jax.random.fold_in(key_of[3], 1), N_TY * N_TX * SD * DD // (SD * DD))
    tile_id_turns = jax.random.permutation(jax.random.fold_in(key_of[3], 3), N_TY * N_TX * SD * DD // (SD * DD))
    tile_id = jax.vmap(lambda own, number: deal_out(jax.random.fold_in(key_of[3], 2), own, number, SD * DD, N_TY * N_TX, 1, CAP, 2))(tile_id_keys, tile_id_turns).reshape((N_TY, N_TX, SD, DD, 1))
    cell_index = place_ends(jax.random.randint(key_of[4], (N_TY, N_TX, SD, DD), 0, (RY - 1) * (RX - P_SIZE - 1)), jax.random.fold_in(key_of[4], 1), 0, ((RY - 1) * (RX - P_SIZE - 1)) - 1).astype(jnp.int32)
    fractions = jnp.clip(1.0 * jax.random.uniform(key_of[5], (2, N_TY, N_TX, SD, DD), jnp.float32) ** level_of(key_of[5], (2, N_TY, N_TX, SD, DD), ((1, 16), (2, 8)), -0.2, 0.2), 0.0, 1.0)
    return {"screen": screen, "wind_table": wind_table, "wind_index": wind_index, "tile_id": tile_id, "cell_index": cell_index, "fractions": fractions}


DIFFUSION = 0.2


def mix(center, east_side, west_side, south_side, north_side, wind_east, wind_south):
    advect = wind_east * (east_side - west_side) + wind_south * (south_side - north_side)
    spread = east_side + west_side + south_side + north_side - 4.0 * center
    return center - 0.5 * advect + DIFFUSION * spread


def strip_values(upper_row, lower_row, frac_row, frac_col):
    left_up = upper_row[..., :-1]
    right_up = upper_row[..., 1:]
    left_low = lower_row[..., :-1]
    right_low = lower_row[..., 1:]
    upper_mix = (1.0 - frac_col) * left_up + frac_col * right_up
    lower_mix = (1.0 - frac_col) * left_low + frac_col * right_low
    phase_vals = (1.0 - frac_row) * upper_mix + frac_row * lower_mix
    slope_vals = (1.0 - frac_col) * (left_low - left_up) + frac_col * (right_low - right_up)
    return phase_vals, slope_vals


def reference(screen, wind_table, wind_index, tile_id, cell_index, fractions):
    east_tile = wind_table[0][wind_index]
    south_tile = wind_table[1][wind_index]
    wind_east = jnp.repeat(jnp.repeat(east_tile, RY, axis=0), RX, axis=1)
    wind_south = jnp.repeat(jnp.repeat(south_tile, RY, axis=0), RX, axis=1)
    field = screen
    for substep in range(SUB):
        padded = jnp.pad(field, 1)
        field = mix(field, padded[1:-1, 2:], padded[1:-1, :-2], padded[2:, 1:-1], padded[:-2, 1:-1], wind_east, wind_south)
    screen_next = field
    span_cols = RX - P_SIZE - 1

    def one_group(inputs):
        tiles_here, cells_here, row_frac, col_frac = inputs
        tiles_flat = tiles_here.reshape(-1).astype(jnp.int32)
        cells_flat = cells_here.reshape(-1).astype(jnp.int32)
        row_start = ((tiles_flat // N_TX) * RY + cells_flat // span_cols).astype(jnp.int32)
        col_start = ((tiles_flat % N_TX) * RX + cells_flat % span_cols).astype(jnp.int32)

        def fetch(row_at, col_at):
            return lax.dynamic_slice(screen_next, (row_at, col_at), (2, P_SIZE + 1))

        blocks = jax.vmap(fetch)(row_start, col_start)
        phase_vals, slope_vals = strip_values(blocks[:, 0], blocks[:, 1], row_frac.reshape(-1, 1), col_frac.reshape(-1, 1))
        return phase_vals, slope_vals

    phase_all, slope_all = lax.map(one_group, (tile_id[..., 0], cell_index, fractions[0], fractions[1]))
    phases = phase_all.reshape(N_TY, N_TX, SD, DD, P_SIZE)
    slopes = slope_all.reshape(N_TY, N_TX, SD, DD, P_SIZE)
    return screen_next, phases, slopes
```

```python
import jax
import jax.numpy as jnp
from jax import lax
from jax.experimental import pallas as pl
from jax.experimental.pallas import tpu as pltpu
from jax.sharding import PartitionSpec as P

RY = 64
RX = 256
P_SIZE = 128
SPAN = RX - P_SIZE - 1
SUB = 4
CAP = 4
DIFFUSION = 0.2

REC = 64
F32 = jnp.float32
BF16 = jnp.bfloat16
VMEM = pl.BlockSpec(memory_space=pltpu.VMEM)
SMEM = pl.BlockSpec(memory_space=pltpu.SMEM)


def iota(shape, dim):
    return lax.broadcasted_iota(jnp.int32, shape, dim)


def three_terms(x):
    high = x.astype(BF16)
    rest = x - high.astype(F32)
    middle = rest.astype(BF16)
    low = (rest - middle.astype(F32)).astype(BF16)
    return high, middle, low


def request_kernel(
    n_tx, screen_ref, table_ref, index_ref, tile_ref, cell_ref, frac_ref,
    send_ref, top_ref, bottom_ref, slot_ref,
):
    tx = lax.axis_index("tx")
    groups, width = tile_ref.shape[0], tile_ref.shape[2]
    records = groups * width
    tiles = send_ref.shape[0] // SUB
    top_ref[...] = screen_ref[0:8, :]
    bottom_ref[...] = screen_ref[RY - 8 : RY, :]

    def flat(rows):
        return jnp.concatenate(rows, axis=1)

    tile = flat([tile_ref[s] for s in range(groups)])
    cell = flat([cell_ref[s : s + 1, :] for s in range(groups)]).astype(F32)
    frac_row = flat([frac_ref[0, s : s + 1, :] for s in range(groups)])
    frac_col = flat([frac_ref[1, s : s + 1, :] for s in range(groups)])

    names = jnp.where(iota((tiles, records), 0) == tile, 1.0, 0.0)
    before = (iota((records, records), 0) < iota((records, records), 1)).astype(F32).astype(BF16)
    earlier = jnp.dot(names.astype(BF16), before, preferred_element_type=F32)
    rank = jnp.sum(names * earlier, axis=0, keepdims=True)
    slot_ref[...] = tile * (2 * CAP) + 2 * rank.astype(jnp.int32)

    picks = jnp.concatenate(
        [jnp.where(earlier == k, names, 0.0).astype(BF16) for k in range(CAP)], axis=0
    )
    line = iota((128, records), 0)
    values = jnp.where(
        line == REC,
        cell,
        jnp.where(line == REC + 1, frac_row, jnp.where(line == REC + 2, frac_col, 0.0)),
    )
    found = sum(
        lax.dot_general(picks, part, (((1,), (1,)), ((), ())), preferred_element_type=F32)
        for part in three_terms(values)
    )
    requests = found[0:tiles]
    for k in range(1, CAP):
        requests = requests + pltpu.roll(found[k * tiles : (k + 1) * tiles], 4 * k, axis=1)

    chosen = jnp.where(iota((2, table_ref.shape[1]), 1) == index_ref[...], table_ref[...], 0.0)
    wind = jnp.sum(chosen, axis=1, keepdims=True)
    lane = iota((1, 128), 1)
    winds = jnp.where(lane == REC, wind[0:1], jnp.where(lane == REC + 1, wind[1:2], 0.0))

    blank = jnp.zeros((128 - RY, 128), F32)
    west_cols = jnp.concatenate([screen_ref[:, 0:128], blank], axis=0).T
    east_cols = jnp.concatenate([screen_ref[:, RX - 128 : RX], blank], axis=0).T
    to_east = lax.rem(iota((tiles, 128), 0), n_tx) == tx + 1
    for c in range(SUB):
        row = jnp.where(
            to_east, east_cols[128 - SUB + c : 129 - SUB + c, :], west_cols[c : c + 1, :]
        )
        if c == 0:
            row = row + requests
        if c == 1:
            row = row + winds
        send_ref[pl.ds(c, tiles, stride=SUB), :] = row


def sample_kernel(
    n_ty, n_tx, screen_ref, north_ref, south_ref, got_ref, next_ref, reply_ref, edge_ref
):
    ty, tx = lax.axis_index("ty"), lax.axis_index("tx")
    tiles = n_ty * n_tx

    def chunk(dy, dx):
        y = jnp.clip(ty + dy, 0, n_ty - 1)
        x = jnp.clip(tx + dx, 0, n_tx - 1)
        return [got_ref[pl.ds((y * n_tx + x) * SUB + c, 1), :] for c in range(SUB)]

    around = {(dy, dx): chunk(dy, dx) for dy in (-1, 0, 1) for dx in (-1, 0, 1)}

    lane = iota((1, 128), 1)
    edge_ref[...] = jnp.zeros((128, 128), F32)
    for dx, start in ((1, 0), (-1, 128 - SUB)):
        for c in range(SUB):
            below = pltpu.roll(around[1, dx][c], RY, axis=1)
            above = pltpu.roll(around[-1, dx][c], 2 * SUB, axis=1)
            edge_ref[start + c : start + c + 1, :] = jnp.where(
                lane < RY, around[0, dx][c], jnp.where(lane < RY + SUB, below, above)
            )
    sides = edge_ref[...].T[0 : RY + 2 * SUB]

    rows, cols = RY + 2 * SUB, RX + 128
    ends = jnp.where(iota((2 * SUB, RX), 0) < SUB, south_ref[...], north_ref[...])
    field = jnp.concatenate(
        [jnp.concatenate([screen_ref[...], ends], axis=0), sides], axis=1
    )
    row, col = iota((rows, cols), 0), iota((rows, cols), 1)
    no_south, no_north = ty == n_ty - 1, ty == 0
    no_east, no_west = tx == n_tx - 1, tx == 0
    first_south = jnp.where(no_south, RY, RY + SUB)
    last_north = jnp.where(no_north, rows, RY + SUB)
    first_east = jnp.where(no_east, RX, RX + REC)
    last_west = jnp.where(no_west, cols, RX + REC)
    inside = ((row < first_south) | (row >= last_north)) & ((col < first_east) | (col >= last_west))

    def spread_wind(which):
        def line(dy):
            w = [around[dy, dx][1][:, REC + which : REC + which + 1] for dx in (0, 1, -1)]
            c = iota((1, cols), 1)
            return jnp.where(c < RX, w[0], jnp.where(c < RX + REC, w[1], w[2]))

        return jnp.where(row < RY, line(0), jnp.where(row < RY + SUB, line(1), line(-1)))

    wind_east, wind_south = spread_wind(0), spread_wind(1)
    field = jnp.where(inside, field, 0.0)
    for _ in range(SUB):
        east, west = pltpu.roll(field, cols - 1, axis=1), pltpu.roll(field, 1, axis=1)
        south, north = pltpu.roll(field, rows - 1, axis=0), pltpu.roll(field, 1, axis=0)
        advect = wind_east * (east - west) + wind_south * (south - north)
        spread = east + west + south + north - 4.0 * field
        field = jnp.where(inside, field - 0.5 * advect + DIFFUSION * spread, 0.0)
    tile = field[0:RY, 0:RX]
    next_ref[...] = tile

    parts = jnp.concatenate(three_terms(tile), axis=0)
    records = got_ref[pl.ds(0, tiles, stride=SUB), :]
    start_row = jnp.floor((records + 0.5) * (1.0 / SPAN))
    start_col = (records - SPAN * start_row).astype(jnp.int32)
    line = lax.rem(iota((tiles, 3 * RY), 1), RY).astype(F32)
    lanes = iota((tiles, 128), 1)
    for k in range(CAP):
        at = REC + 4 * k
        row_k, col_k = start_row[:, at : at + 1], start_col[:, at : at + 1]
        frac_row, frac_col = records[:, at + 1 : at + 2], records[:, at + 2 : at + 3]
        upper = jnp.dot(
            jnp.where(line == row_k, 1.0, 0.0).astype(BF16), parts, preferred_element_type=F32
        )
        lower = jnp.dot(
            jnp.where(line == row_k + 1.0, 1.0, 0.0).astype(BF16), parts, preferred_element_type=F32
        )
        spot = lanes + col_k
        near = spot < 128
        spot = spot & 127
        for p, value in enumerate(((1.0 - frac_row) * upper + frac_row * lower, lower - upper)):
            value = (1.0 - frac_col) * value + frac_col * pltpu.roll(value, RX - 1, axis=1)
            strip = jnp.where(
                near,
                jnp.take_along_axis(value[:, 0:128], spot, axis=1),
                jnp.take_along_axis(value[:, 128:256], spot, axis=1),
            )
            reply_ref[pl.ds(2 * k + p, tiles, stride=2 * CAP), :] = strip


def collect_kernel(slot_ref, got_ref, phase_ref, slope_ref):
    def step(n, carry):
        slot = slot_ref[0, n]
        phase_ref[pl.ds(n, 1), :] = got_ref[pl.ds(slot, 1), :]
        slope_ref[pl.ds(n, 1), :] = got_ref[pl.ds(slot + 1, 1), :]
        return carry

    lax.fori_loop(0, phase_ref.shape[0], step, 0, unroll=8)


def local(screen, wind_table, wind_index, tile_id, cell_index, fractions):
    n_ty, n_tx = lax.axis_size("ty"), lax.axis_size("tx")
    tiles = n_ty * n_tx
    groups, width = tile_id.shape[2], tile_id.shape[3]
    records = groups * width

    def shaped(*shape, dtype=F32):
        return jax.ShapeDtypeStruct(shape, dtype)

    send, top, bottom, slots = pl.pallas_call(
        lambda *refs: request_kernel(n_tx, *refs),
        out_shape=(
            shaped(tiles * SUB, 128),
            shaped(8, RX),
            shaped(8, RX),
            shaped(1, records, dtype=jnp.int32),
        ),
        in_specs=[VMEM] * 6,
        out_specs=(VMEM,) * 4,
        name="make_requests",
    )(
        screen,
        wind_table,
        wind_index,
        tile_id.reshape(groups, 1, width),
        cell_index.reshape(groups, width),
        fractions.reshape(2, groups, width),
    )

    def exchange(x):
        return lax.all_to_all(x, ("ty", "tx"), split_axis=0, concat_axis=0, tiled=True)

    got = exchange(send)
    north = lax.ppermute(bottom, "ty", [(i, i + 1) for i in range(n_ty - 1)])
    south = lax.ppermute(top, "ty", [(i + 1, i) for i in range(n_ty - 1)])
    screen_next, reply = pl.pallas_call(
        lambda *refs: sample_kernel(n_ty, n_tx, *refs),
        out_shape=(shaped(RY, RX), shaped(tiles * 2 * CAP, 128)),
        in_specs=[VMEM] * 4,
        out_specs=(VMEM,) * 2,
        scratch_shapes=[pltpu.VMEM((128, 128), F32)],
        name="step_and_sample",
    )(screen, north, south, got)
    returned = exchange(reply)
    phases, slopes = pl.pallas_call(
        collect_kernel,
        out_shape=(shaped(records, P_SIZE),) * 2,
        in_specs=[SMEM, VMEM],
        out_specs=(VMEM,) * 2,
        name="collect",
    )(slots, returned)
    out_shape = (1, 1, groups, width, P_SIZE)
    return screen_next, phases.reshape(out_shape), slopes.reshape(out_shape)


def solution(mesh):
    in_specs = (
        P("ty", "tx"),
        P(),
        P("ty", "tx"),
        P("ty", "tx", None, None, None),
        P("ty", "tx", None, None),
        P(None, "ty", "tx", None, None),
    )
    out_specs = (P("ty", "tx"), P("ty", "tx", None, None, None), P("ty", "tx", None, None, None))
    return jax.shard_map(local, mesh=mesh, in_specs=in_specs, out_specs=out_specs, check_vma=False)
```

```python
import jax
import jax.numpy as jnp
from jax import lax
from jax.experimental import pallas as pl
from jax.experimental.pallas import tpu as pltpu
from jax.sharding import PartitionSpec as P

RY = 64
RX = 256
P_SIZE = 128
SPAN = RX - P_SIZE - 1
SUB = 4
CAP = 4
DIFFUSION = 0.2

REC = 64
F32 = jnp.float32
BF16 = jnp.bfloat16
VMEM = pl.BlockSpec(memory_space=pltpu.VMEM)
SMEM = pl.BlockSpec(memory_space=pltpu.SMEM)
HBM = pl.BlockSpec(memory_space=pltpu.HBM)
PARAMS = pltpu.CompilerParams(vmem_limit_bytes=8 << 20)


def iota(shape, dim):
    return lax.broadcasted_iota(jnp.int32, shape, dim)


def three_terms(x):
    high = x.astype(BF16)
    rest = x - high.astype(F32)
    middle = rest.astype(BF16)
    low = (rest - middle.astype(F32)).astype(BF16)
    return high, middle, low


def request_kernel(n_tx, index_ref, *refs):
    sources, refs = refs[:5], refs[5:]
    (send_ref, edge_ref, slot_ref), refs = refs[:3], refs[3:]
    copies = [pltpu.make_async_copy(sources[i], refs[i], refs[5].at[i]) for i in range(5)]
    for copy in copies:
        copy.start()
    screen_ref, table_ref, tile_ref, cell_ref, frac_ref = refs[:5]
    for copy in copies:
        copy.wait()
    tx = lax.axis_index("tx")
    groups, width = tile_ref.shape[0], tile_ref.shape[2]
    records = groups * width
    tiles = send_ref.shape[0] // SUB
    edge_ref[...] = jnp.where(
        iota((2 * SUB, RX), 0) < SUB, screen_ref[0 : 2 * SUB, :], screen_ref[RY - 2 * SUB : RY, :]
    )

    def flat(rows):
        return jnp.concatenate(rows, axis=1)

    tile = flat([tile_ref[s] for s in range(groups)])
    cell = flat([cell_ref[s : s + 1, :] for s in range(groups)]).astype(F32)
    frac_row = flat([frac_ref[0, s : s + 1, :] for s in range(groups)])
    frac_col = flat([frac_ref[1, s : s + 1, :] for s in range(groups)])

    names = jnp.where(iota((tiles, records), 0) == tile, 1.0, 0.0)
    before = (iota((records, records), 0) < iota((records, records), 1)).astype(F32).astype(BF16)
    earlier = jnp.dot(names.astype(BF16), before, preferred_element_type=F32)
    rank = jnp.sum(names * earlier, axis=0, keepdims=True)
    slot_ref[...] = tile * (2 * CAP) + 2 * rank.astype(jnp.int32)

    picks = jnp.concatenate(
        [jnp.where(earlier == k, names, 0.0).astype(BF16) for k in range(CAP)], axis=0
    )
    line = iota((128, records), 0)
    values = jnp.where(
        line == REC,
        cell,
        jnp.where(line == REC + 1, frac_row, jnp.where(line == REC + 2, frac_col, 0.0)),
    )
    found = sum(
        lax.dot_general(picks, part, (((1,), (1,)), ((), ())), preferred_element_type=F32)
        for part in three_terms(values)
    )
    requests = found[0:tiles]
    for k in range(1, CAP):
        requests = requests + pltpu.roll(found[k * tiles : (k + 1) * tiles], 4 * k, axis=1)

    chosen = jnp.where(iota((2, table_ref.shape[1]), 1) == index_ref[0, 0], table_ref[...], 0.0)
    wind = jnp.sum(chosen, axis=1, keepdims=True)
    lane = iota((1, 128), 1)
    winds = jnp.where(lane == REC, wind[0:1], jnp.where(lane == REC + 1, wind[1:2], 0.0))

    blank = jnp.zeros((128 - RY, 128), F32)
    west_cols = jnp.concatenate([screen_ref[:, 0:128], blank], axis=0).T
    east_cols = jnp.concatenate([screen_ref[:, RX - 128 : RX], blank], axis=0).T
    to_east = lax.rem(iota((tiles, 128), 0), n_tx) == tx + 1
    for c in range(SUB):
        row = jnp.where(
            to_east, east_cols[128 - SUB + c : 129 - SUB + c, :], west_cols[c : c + 1, :]
        )
        if c == 0:
            row = row + requests
        if c == 1:
            row = row + winds
        send_ref[pl.ds(c, tiles, stride=SUB), :] = row


def sample_kernel(
    n_ty, n_tx, screen_ref, inner_ref, outer_ref, got_ref, next_ref, reply_ref, edge_ref
):
    ty, tx = lax.axis_index("ty"), lax.axis_index("tx")
    tiles = n_ty * n_tx

    def chunk(dy, dx):
        y = jnp.clip(ty + dy, 0, n_ty - 1)
        x = jnp.clip(tx + dx, 0, n_tx - 1)
        return [got_ref[pl.ds((y * n_tx + x) * SUB + c, 1), :] for c in range(SUB)]

    around = {(dy, dx): chunk(dy, dx) for dy in (-1, 0, 1) for dx in (-1, 0, 1)}

    lane = iota((1, 128), 1)
    edge_ref[...] = jnp.zeros((128, 128), F32)
    for dx, start in ((1, 0), (-1, 128 - SUB)):
        for c in range(SUB):
            below = pltpu.roll(around[1, dx][c], RY, axis=1)
            above = pltpu.roll(around[-1, dx][c], 2 * SUB, axis=1)
            edge_ref[start + c : start + c + 1, :] = jnp.where(
                lane < RY, around[0, dx][c], jnp.where(lane < RY + SUB, below, above)
            )
    sides = edge_ref[...].T[0 : RY + 2 * SUB]

    rows, cols = RY + 2 * SUB, RX + 128
    even = lax.rem(ty, 2) == 0
    ends = jnp.where((iota((2 * SUB, RX), 0) < SUB) == even, inner_ref[...], outer_ref[...])
    field = jnp.concatenate(
        [jnp.concatenate([screen_ref[...], ends], axis=0), sides], axis=1
    )
    row, col = iota((rows, cols), 0), iota((rows, cols), 1)
    no_south, no_north = ty == n_ty - 1, ty == 0
    no_east, no_west = tx == n_tx - 1, tx == 0
    first_south = jnp.where(no_south, RY, RY + SUB)
    last_north = jnp.where(no_north, rows, RY + SUB)
    first_east = jnp.where(no_east, RX, RX + REC)
    last_west = jnp.where(no_west, cols, RX + REC)
    inside = ((row < first_south) | (row >= last_north)) & ((col < first_east) | (col >= last_west))

    def spread_wind(which):
        def line(dy):
            w = [around[dy, dx][1][:, REC + which : REC + which + 1] for dx in (0, 1, -1)]
            c = iota((1, cols), 1)
            return jnp.where(c < RX, w[0], jnp.where(c < RX + REC, w[1], w[2]))

        return jnp.where(row < RY, line(0), jnp.where(row < RY + SUB, line(1), line(-1)))

    wind_east, wind_south = spread_wind(0), spread_wind(1)
    field = jnp.where(inside, field, 0.0)
    for _ in range(SUB):
        east, west = pltpu.roll(field, cols - 1, axis=1), pltpu.roll(field, 1, axis=1)
        south, north = pltpu.roll(field, rows - 1, axis=0), pltpu.roll(field, 1, axis=0)
        advect = wind_east * (east - west) + wind_south * (south - north)
        spread = east + west + south + north - 4.0 * field
        field = jnp.where(inside, field - 0.5 * advect + DIFFUSION * spread, 0.0)
    tile = field[0:RY, 0:RX]
    next_ref[...] = tile

    parts = jnp.concatenate(three_terms(tile), axis=0)
    records = got_ref[pl.ds(0, tiles, stride=SUB), :]
    start_row = jnp.floor((records + 0.5) * (1.0 / SPAN))
    start_col = (records - SPAN * start_row).astype(jnp.int32)
    line = lax.rem(iota((tiles, 3 * RY), 1), RY).astype(F32)
    lanes = iota((tiles, 128), 1)
    for k in range(CAP):
        at = REC + 4 * k
        row_k, col_k = start_row[:, at : at + 1], start_col[:, at : at + 1]
        frac_row, frac_col = records[:, at + 1 : at + 2], records[:, at + 2 : at + 3]
        upper = jnp.dot(
            jnp.where(line == row_k, 1.0, 0.0).astype(BF16), parts, preferred_element_type=F32
        )
        lower = jnp.dot(
            jnp.where(line == row_k + 1.0, 1.0, 0.0).astype(BF16), parts, preferred_element_type=F32
        )
        spot = lanes + col_k
        near = spot < 128
        spot = spot & 127
        for p, value in enumerate(((1.0 - frac_row) * upper + frac_row * lower, lower - upper)):
            value = (1.0 - frac_col) * value + frac_col * pltpu.roll(value, RX - 1, axis=1)
            strip = jnp.where(
                near,
                jnp.take_along_axis(value[:, 0:128], spot, axis=1),
                jnp.take_along_axis(value[:, 128:256], spot, axis=1),
            )
            reply_ref[pl.ds(2 * k + p, tiles, stride=2 * CAP), :] = strip


def collect_kernel(slot_ref, got_ref, phase_ref, slope_ref):
    def step(n, carry):
        slot = slot_ref[0, n]
        phase_ref[pl.ds(n, 1), :] = got_ref[pl.ds(slot, 1), :]
        slope_ref[pl.ds(n, 1), :] = got_ref[pl.ds(slot + 1, 1), :]
        return carry

    lax.fori_loop(0, phase_ref.shape[0], step, 0, unroll=8)


def local(screen, wind_table, wind_index, tile_id, cell_index, fractions):
    n_ty, n_tx = lax.axis_size("ty"), lax.axis_size("tx")
    tiles = n_ty * n_tx
    groups, width = tile_id.shape[2], tile_id.shape[3]
    records = groups * width

    def shaped(*shape, dtype=F32):
        return jax.ShapeDtypeStruct(shape, dtype)

    send, edges, slots = pl.pallas_call(
        lambda *refs: request_kernel(n_tx, *refs),
        out_shape=(
            shaped(tiles * SUB, 128),
            shaped(2 * SUB, RX),
            shaped(1, records, dtype=jnp.int32),
        ),
        in_specs=[SMEM] + [HBM] * 5,
        out_specs=(VMEM,) * 3,
        scratch_shapes=[
            pltpu.VMEM((RY, RX), F32),
            pltpu.VMEM(wind_table.shape, F32),
            pltpu.VMEM((groups, 1, width), jnp.int32),
            pltpu.VMEM((groups, width), jnp.int32),
            pltpu.VMEM((2, groups, width), F32),
            pltpu.SemaphoreType.DMA((5,)),
        ],
        compiler_params=PARAMS,
        name="make_requests",
    )(
        wind_index,
        *[
            pltpu.with_memory_space_constraint(x, pltpu.HBM)
            for x in (
                screen,
                wind_table,
                tile_id.reshape(groups, 1, width),
                cell_index.reshape(groups, width),
                fractions.reshape(2, groups, width),
            )
        ],
    )

    def exchange(x):
        return lax.all_to_all(x, ("ty", "tx"), split_axis=0, concat_axis=0, tiled=True)

    got = exchange(send)
    def swap(first):
        pairs = [(i, i + 1) for i in range(first, n_ty - 1, 2)]
        return lax.ppermute(edges, "ty", pairs + [(j, i) for i, j in pairs])

    inner, outer = swap(0), swap(1)
    screen_next, reply = pl.pallas_call(
        lambda *refs: sample_kernel(n_ty, n_tx, *refs),
        out_shape=(shaped(RY, RX), shaped(tiles * 2 * CAP, 128)),
        in_specs=[VMEM] * 4,
        out_specs=(VMEM,) * 2,
        scratch_shapes=[pltpu.VMEM((128, 128), F32)],
        compiler_params=PARAMS,
        name="step_and_sample",
    )(screen, inner, outer, got)
    returned = exchange(reply)
    phases, slopes = pl.pallas_call(
        collect_kernel,
        out_shape=(shaped(records, P_SIZE),) * 2,
        in_specs=[SMEM, VMEM],
        out_specs=(VMEM,) * 2,
        compiler_params=PARAMS,
        name="collect",
    )(slots, returned)
    out_shape = (1, 1, groups, width, P_SIZE)
    return screen_next, phases.reshape(out_shape), slopes.reshape(out_shape)


def solution(mesh):
    in_specs = (
        P("ty", "tx"),
        P(),
        P("ty", "tx"),
        P("ty", "tx", None, None, None),
        P("ty", "tx", None, None),
        P(None, "ty", "tx", None, None),
    )
    out_specs = (P("ty", "tx"), P("ty", "tx", None, None, None), P("ty", "tx", None, None, None))
    return jax.shard_map(local, mesh=mesh, in_specs=in_specs, out_specs=out_specs, check_vma=False)
```

```python
import jax
import jax.numpy as jnp
from jax import lax
from jax.experimental import pallas as pl
from jax.experimental.pallas import tpu as pltpu
from jax.sharding import PartitionSpec as P

RY = 64
RX = 256
P_SIZE = 128
SPAN = RX - P_SIZE - 1
SUB = 4
CAP = 4
DIFFUSION = 0.2
PARTS = 2
UNROLL = 32

REC = 64
F32 = jnp.float32
BF16 = jnp.bfloat16
VMEM = pl.BlockSpec(memory_space=pltpu.VMEM)
SMEM = pl.BlockSpec(memory_space=pltpu.SMEM)
HBM = pl.BlockSpec(memory_space=pltpu.HBM)
PARAMS = pltpu.CompilerParams(vmem_limit_bytes=8 << 20)


def iota(shape, dim):
    return lax.broadcasted_iota(jnp.int32, shape, dim)


def three_terms(x):
    high = x.astype(BF16)
    rest = x - high.astype(F32)
    middle = rest.astype(BF16)
    low = (rest - middle.astype(F32)).astype(BF16)
    return high, middle, low


def request_kernel(n_tx, index_ref, *refs):
    sources, refs = refs[:5], refs[5:]
    (send_ref, edge_ref, slot_out), refs = refs[:3], refs[3:]
    (slot_ref, slot_sem), refs = refs[:2], refs[2:]
    copies = [pltpu.make_async_copy(sources[i], refs[i], refs[5].at[i]) for i in range(5)]
    for copy in copies:
        copy.start()
    screen_ref, table_ref, tile_ref, cell_ref, frac_ref = refs[:5]
    tx = lax.axis_index("tx")
    groups, width = tile_ref.shape[0], tile_ref.shape[2]
    records = groups * width
    tiles = send_ref.shape[0] // SUB
    before = (iota((records, records), 0) < iota((records, records), 1)).astype(F32).astype(BF16)
    for copy in copies[2:]:
        copy.wait()

    def flat(rows):
        return jnp.concatenate(rows, axis=1)

    tile = flat([tile_ref[s] for s in range(groups)])
    cell = flat([cell_ref[s : s + 1, :] for s in range(groups)]).astype(F32)
    frac_row = flat([frac_ref[0, s : s + 1, :] for s in range(groups)])
    frac_col = flat([frac_ref[1, s : s + 1, :] for s in range(groups)])

    names = jnp.where(iota((tiles, records), 0) == tile, 1.0, 0.0)
    earlier = jnp.dot(names.astype(BF16), before, preferred_element_type=F32)
    rank = jnp.sum(names * earlier, axis=0, keepdims=True)
    slot_ref[...] = tile * (2 * CAP) + 2 * rank.astype(jnp.int32)
    slots = pltpu.make_async_copy(slot_ref, slot_out, slot_sem)
    slots.start()

    picks = jnp.concatenate(
        [jnp.where(earlier == k, names, 0.0).astype(BF16) for k in range(CAP)], axis=0
    )
    line = iota((128, records), 0)
    values = jnp.where(
        line == REC,
        cell,
        jnp.where(line == REC + 1, frac_row, jnp.where(line == REC + 2, frac_col, 0.0)),
    )
    found = sum(
        lax.dot_general(picks, part, (((1,), (1,)), ((), ())), preferred_element_type=F32)
        for part in three_terms(values)
    )
    requests = found[0:tiles]
    for k in range(1, CAP):
        requests = requests + pltpu.roll(found[k * tiles : (k + 1) * tiles], 4 * k, axis=1)

    for copy in copies[:2]:
        copy.wait()
    edge_ref[...] = jnp.where(
        iota((2 * SUB, RX), 0) < SUB, screen_ref[0 : 2 * SUB, :], screen_ref[RY - 2 * SUB : RY, :]
    )
    chosen = jnp.where(iota((2, table_ref.shape[1]), 1) == index_ref[0, 0], table_ref[...], 0.0)
    wind = jnp.sum(chosen, axis=1, keepdims=True)
    lane = iota((1, 128), 1)
    winds = jnp.where(lane == REC, wind[0:1], jnp.where(lane == REC + 1, wind[1:2], 0.0))

    blank = jnp.zeros((128 - RY, 128), F32)
    west_cols = jnp.concatenate([screen_ref[:, 0:128], blank], axis=0).T
    east_cols = jnp.concatenate([screen_ref[:, RX - 128 : RX], blank], axis=0).T
    to_east = lax.rem(iota((tiles, 128), 0), n_tx) == tx + 1
    for c in range(SUB):
        row = jnp.where(
            to_east, east_cols[128 - SUB + c : 129 - SUB + c, :], west_cols[c : c + 1, :]
        )
        if c == 0:
            row = row + requests
        if c == 1:
            row = row + winds
        send_ref[pl.ds(c, tiles, stride=SUB), :] = row
    slots.wait()


def sample_kernel(
    n_ty, n_tx, screen_ref, inner_ref, outer_ref, got_ref, next_ref, reply_ref, edge_ref, tile_ref, sem
):
    ty, tx = lax.axis_index("ty"), lax.axis_index("tx")
    tiles = n_ty * n_tx

    def chunk(dy, dx):
        y = jnp.clip(ty + dy, 0, n_ty - 1)
        x = jnp.clip(tx + dx, 0, n_tx - 1)
        return [got_ref[pl.ds((y * n_tx + x) * SUB + c, 1), :] for c in range(SUB)]

    around = {(dy, dx): chunk(dy, dx) for dy in (-1, 0, 1) for dx in (-1, 0, 1)}

    lane = iota((1, 128), 1)
    edge_ref[...] = jnp.zeros((128, 128), F32)
    for dx, start in ((1, 0), (-1, 128 - SUB)):
        for c in range(SUB):
            below = pltpu.roll(around[1, dx][c], RY, axis=1)
            above = pltpu.roll(around[-1, dx][c], 2 * SUB, axis=1)
            edge_ref[start + c : start + c + 1, :] = jnp.where(
                lane < RY, around[0, dx][c], jnp.where(lane < RY + SUB, below, above)
            )
    sides = edge_ref[...].T[0 : RY + 2 * SUB]

    rows, cols = RY + 2 * SUB, RX + 128
    even = lax.rem(ty, 2) == 0
    ends = jnp.where((iota((2 * SUB, RX), 0) < SUB) == even, inner_ref[...], outer_ref[...])
    field = jnp.concatenate(
        [jnp.concatenate([screen_ref[...], ends], axis=0), sides], axis=1
    )
    row, col = iota((rows, cols), 0), iota((rows, cols), 1)
    no_south, no_north = ty == n_ty - 1, ty == 0
    no_east, no_west = tx == n_tx - 1, tx == 0
    first_south = jnp.where(no_south, RY, RY + SUB)
    last_north = jnp.where(no_north, rows, RY + SUB)
    first_east = jnp.where(no_east, RX, RX + REC)
    last_west = jnp.where(no_west, cols, RX + REC)
    inside = ((row < first_south) | (row >= last_north)) & ((col < first_east) | (col >= last_west))

    def spread_wind(which):
        def line(dy):
            w = [around[dy, dx][1][:, REC + which : REC + which + 1] for dx in (0, 1, -1)]
            c = iota((1, cols), 1)
            return jnp.where(c < RX, w[0], jnp.where(c < RX + REC, w[1], w[2]))

        return jnp.where(row < RY, line(0), jnp.where(row < RY + SUB, line(1), line(-1)))

    wind_east, wind_south = spread_wind(0), spread_wind(1)
    field = jnp.where(inside, field, 0.0)
    for _ in range(SUB):
        east, west = pltpu.roll(field, cols - 1, axis=1), pltpu.roll(field, 1, axis=1)
        south, north = pltpu.roll(field, rows - 1, axis=0), pltpu.roll(field, 1, axis=0)
        advect = wind_east * (east - west) + wind_south * (south - north)
        spread = east + west + south + north - 4.0 * field
        field = jnp.where(inside, field - 0.5 * advect + DIFFUSION * spread, 0.0)
    tile = field[0:RY, 0:RX]
    tile_ref[...] = tile
    store = pltpu.make_async_copy(tile_ref, next_ref, sem)
    store.start()

    both = jnp.concatenate([tile, pltpu.roll(tile, RX - 1, axis=1)], axis=1)
    parts = jnp.concatenate(three_terms(both), axis=0)
    records = got_ref[pl.ds(0, tiles, stride=SUB), :]
    line = lax.rem(iota((tiles, 3 * RY), 1), RY).astype(F32)
    lanes = iota((tiles, 128), 1)
    for k in range(CAP):
        at = REC + 4 * k
        cell, frac_row, frac_col = [records[:, at + v : at + v + 1] for v in range(3)]
        cell = jnp.broadcast_to(cell, (tiles, 128))
        row_k = jnp.floor((cell + 0.5) * (1.0 / SPAN))
        col_k = (cell - SPAN * row_k).astype(jnp.int32)
        row_k = jnp.concatenate([row_k, row_k[:, 0 : 3 * RY - 128]], axis=1)
        upper, lower = [
            jnp.dot(
                jnp.where(line == row_k + d, 1.0, 0.0).astype(BF16), parts, preferred_element_type=F32
            )
            for d in (0.0, 1.0)
        ]
        far = lanes < col_k
        spot = (lanes + col_k) & 127
        upper, lower = [
            [
                jnp.where(far, value[:, at + 128 : at + 256], value[:, at : at + 128])
                for at in (0, RX)
            ]
            for value in (upper, lower)
        ]
        rows = [(1.0 - frac_row) * upper[i] + frac_row * lower[i] for i in range(2)]
        steps = [lower[i] - upper[i] for i in range(2)]
        for p, (left, right) in enumerate((rows, steps)):
            value = (1.0 - frac_col) * left + frac_col * right
            reply_ref[pl.ds(2 * k + p, tiles, stride=2 * CAP), :] = jnp.take_along_axis(
                value, spot, axis=1
            )
    store.wait()


def collect_kernel(slot_ref, got_ref, phase_ref, slope_ref, phase_rows, slope_rows, sems):
    records = phase_rows.shape[0]
    part = records // PARTS
    stores = []
    for p in range(PARTS):

        def step(n, carry):
            slot = slot_ref[0, n]
            phase_rows[pl.ds(n, 1), :] = got_ref[pl.ds(slot, 1), :]
            slope_rows[pl.ds(n, 1), :] = got_ref[pl.ds(slot + 1, 1), :]
            return carry

        lax.fori_loop(p * part, (p + 1) * part, step, 0, unroll=UNROLL)
        for i, (rows, out) in enumerate(((phase_rows, phase_ref), (slope_rows, slope_ref))):
            here = pl.ds(p * part, part)
            stores.append(pltpu.make_async_copy(rows.at[here], out.at[here], sems.at[2 * p + i]))
            stores[-1].start()
    for store in stores:
        store.wait()


def local(screen, wind_table, wind_index, tile_id, cell_index, fractions):
    n_ty, n_tx = lax.axis_size("ty"), lax.axis_size("tx")
    tiles = n_ty * n_tx
    groups, width = tile_id.shape[2], tile_id.shape[3]
    records = groups * width

    def shaped(*shape, dtype=F32):
        return jax.ShapeDtypeStruct(shape, dtype)

    send, edges, slots = pl.pallas_call(
        lambda *refs: request_kernel(n_tx, *refs),
        out_shape=(
            shaped(tiles * SUB, 128),
            shaped(2 * SUB, RX),
            pltpu.SMEM((1, records), jnp.int32),
        ),
        in_specs=[SMEM] + [HBM] * 5,
        out_specs=(VMEM, VMEM, SMEM),
        scratch_shapes=[
            pltpu.VMEM((1, records), jnp.int32),
            pltpu.SemaphoreType.DMA,
            pltpu.VMEM((RY, RX), F32),
            pltpu.VMEM(wind_table.shape, F32),
            pltpu.VMEM((groups, 1, width), jnp.int32),
            pltpu.VMEM((groups, width), jnp.int32),
            pltpu.VMEM((2, groups, width), F32),
            pltpu.SemaphoreType.DMA((5,)),
        ],
        compiler_params=PARAMS,
        name="make_requests",
    )(
        wind_index,
        *[
            pltpu.with_memory_space_constraint(x, pltpu.HBM)
            for x in (
                screen,
                wind_table,
                tile_id.reshape(groups, 1, width),
                cell_index.reshape(groups, width),
                fractions.reshape(2, groups, width),
            )
        ],
    )

    def exchange(x):
        return lax.all_to_all(x, ("ty", "tx"), split_axis=0, concat_axis=0, tiled=True)

    got = exchange(send)
    def swap(first):
        pairs = [(i, i + 1) for i in range(first, n_ty - 1, 2)]
        return lax.ppermute(edges, "ty", pairs + [(j, i) for i, j in pairs])

    inner, outer = swap(0), swap(1)
    screen_next, reply = pl.pallas_call(
        lambda *refs: sample_kernel(n_ty, n_tx, *refs),
        out_shape=(shaped(RY, RX), shaped(tiles * 2 * CAP, 128)),
        in_specs=[VMEM] * 4,
        out_specs=(HBM, VMEM),
        scratch_shapes=[
            pltpu.VMEM((128, 128), F32),
            pltpu.VMEM((RY, RX), F32),
            pltpu.SemaphoreType.DMA,
        ],
        compiler_params=PARAMS,
        name="step_and_sample",
    )(screen, inner, outer, got)
    returned = exchange(reply)
    phases, slopes = pl.pallas_call(
        collect_kernel,
        out_shape=(shaped(records, P_SIZE),) * 2,
        in_specs=[SMEM, VMEM],
        out_specs=(HBM,) * 2,
        scratch_shapes=[
            pltpu.VMEM((records, P_SIZE), F32),
            pltpu.VMEM((records, P_SIZE), F32),
            pltpu.SemaphoreType.DMA((2 * PARTS,)),
        ],
        compiler_params=PARAMS,
        name="collect",
    )(slots, returned)
    out_shape = (1, 1, groups, width, P_SIZE)
    return screen_next, phases.reshape(out_shape), slopes.reshape(out_shape)


def solution(mesh):
    in_specs = (
        P("ty", "tx"),
        P(),
        P("ty", "tx"),
        P("ty", "tx", None, None, None),
        P("ty", "tx", None, None),
        P(None, "ty", "tx", None, None),
    )
    out_specs = (P("ty", "tx"), P("ty", "tx", None, None, None), P("ty", "tx", None, None, None))
    return jax.shard_map(local, mesh=mesh, in_specs=in_specs, out_specs=out_specs, check_vma=False)
```

```python
import jax
import jax.numpy as jnp
from jax import lax
from jax.experimental import pallas as pl
from jax.experimental.pallas import tpu as pltpu
from jax.sharding import PartitionSpec as P

RY = 64
RX = 256
P_SIZE = 128
SPAN = RX - P_SIZE - 1
SUB = 4
CAP = 4
DIFFUSION = 0.2
PARTS = 2
UNROLL = 32

REC = 64
F32 = jnp.float32
BF16 = jnp.bfloat16
VMEM = pl.BlockSpec(memory_space=pltpu.VMEM)
SMEM = pl.BlockSpec(memory_space=pltpu.SMEM)
HBM = pl.BlockSpec(memory_space=pltpu.HBM)
PARAMS = pltpu.CompilerParams(vmem_limit_bytes=8 << 20)


def iota(shape, dim):
    return lax.broadcasted_iota(jnp.int32, shape, dim)


def three_terms(x):
    high = x.astype(BF16)
    rest = x - high.astype(F32)
    middle = rest.astype(BF16)
    low = (rest - middle.astype(F32)).astype(BF16)
    return high, middle, low


def request_kernel(n_tx, index_ref, tile_ref, *refs):
    sources, refs = refs[:4], refs[4:]
    (send_ref, edge_ref, slot_out), refs = refs[:3], refs[3:]
    (slot_ref, slot_sem), refs = refs[:2], refs[2:]
    copies = [pltpu.make_async_copy(sources[i], refs[i], refs[4].at[i]) for i in range(4)]
    for copy in copies:
        copy.start()
    screen_ref, table_ref, cell_ref, frac_ref = refs[:4]
    tx = lax.axis_index("tx")
    groups, width = tile_ref.shape[0], tile_ref.shape[2]
    records = groups * width
    tiles = send_ref.shape[0] // SUB
    before = (iota((records, records), 0) < iota((records, records), 1)).astype(F32).astype(BF16)

    def flat(rows):
        return jnp.concatenate(rows, axis=1)

    tile = flat([tile_ref[s] for s in range(groups)])
    names = jnp.where(iota((tiles, records), 0) == tile, 1.0, 0.0)
    earlier = jnp.dot(names.astype(BF16), before, preferred_element_type=F32)
    rank = jnp.sum(names * earlier, axis=0, keepdims=True)
    slot_ref[...] = tile * (2 * CAP) + 2 * rank.astype(jnp.int32)
    slots = pltpu.make_async_copy(slot_ref, slot_out, slot_sem)
    slots.start()

    picks = jnp.concatenate(
        [jnp.where(earlier == k, names, 0.0).astype(BF16) for k in range(CAP)], axis=0
    )
    for copy in copies[2:]:
        copy.wait()
    cell = flat([cell_ref[s : s + 1, :] for s in range(groups)]).astype(F32)
    frac_row = flat([frac_ref[0, s : s + 1, :] for s in range(groups)])
    frac_col = flat([frac_ref[1, s : s + 1, :] for s in range(groups)])
    line = iota((128, records), 0)
    values = jnp.where(
        line == REC,
        cell,
        jnp.where(line == REC + 1, frac_row, jnp.where(line == REC + 2, frac_col, 0.0)),
    )
    found = sum(
        lax.dot_general(picks, part, (((1,), (1,)), ((), ())), preferred_element_type=F32)
        for part in three_terms(values)
    )
    requests = found[0:tiles]
    for k in range(1, CAP):
        requests = requests + pltpu.roll(found[k * tiles : (k + 1) * tiles], 4 * k, axis=1)

    for copy in copies[:2]:
        copy.wait()
    edge_ref[...] = jnp.where(
        iota((2 * SUB, RX), 0) < SUB, screen_ref[0 : 2 * SUB, :], screen_ref[RY - 2 * SUB : RY, :]
    )
    chosen = jnp.where(iota((2, table_ref.shape[1]), 1) == index_ref[0, 0], table_ref[...], 0.0)
    wind = jnp.sum(chosen, axis=1, keepdims=True)
    lane = iota((1, 128), 1)
    winds = jnp.where(lane == REC, wind[0:1], jnp.where(lane == REC + 1, wind[1:2], 0.0))

    blank = jnp.zeros((128 - RY, 128), F32)
    west_cols = jnp.concatenate([screen_ref[:, 0:128], blank], axis=0).T
    east_cols = jnp.concatenate([screen_ref[:, RX - 128 : RX], blank], axis=0).T
    to_east = lax.rem(iota((tiles, 128), 0), n_tx) == tx + 1
    for c in range(SUB):
        row = jnp.where(
            to_east, east_cols[128 - SUB + c : 129 - SUB + c, :], west_cols[c : c + 1, :]
        )
        if c == 0:
            row = row + requests
        if c == 1:
            row = row + winds
        send_ref[pl.ds(c, tiles, stride=SUB), :] = row
    slots.wait()


def sample_kernel(
    n_ty, n_tx, screen_ref, inner_ref, outer_ref, got_ref, next_ref, reply_ref, edge_ref, tile_ref, sem
):
    ty, tx = lax.axis_index("ty"), lax.axis_index("tx")
    tiles = n_ty * n_tx

    def chunk(dy, dx):
        y = jnp.clip(ty + dy, 0, n_ty - 1)
        x = jnp.clip(tx + dx, 0, n_tx - 1)
        return [got_ref[pl.ds((y * n_tx + x) * SUB + c, 1), :] for c in range(SUB)]

    around = {(dy, dx): chunk(dy, dx) for dy in (-1, 0, 1) for dx in (-1, 0, 1)}

    lane = iota((1, 128), 1)
    edge_ref[...] = jnp.zeros((128, 128), F32)
    for dx, start in ((1, 0), (-1, 128 - SUB)):
        for c in range(SUB):
            below = pltpu.roll(around[1, dx][c], RY, axis=1)
            above = pltpu.roll(around[-1, dx][c], 2 * SUB, axis=1)
            edge_ref[start + c : start + c + 1, :] = jnp.where(
                lane < RY, around[0, dx][c], jnp.where(lane < RY + SUB, below, above)
            )
    sides = edge_ref[...].T[0 : RY + 2 * SUB]

    rows, cols = RY + 2 * SUB, RX + 128
    ends = jnp.where((iota((2 * SUB, RX), 0) < SUB) , inner_ref[...], outer_ref[...])
    field = jnp.concatenate(
        [jnp.concatenate([screen_ref[...], ends], axis=0), sides], axis=1
    )
    row, col = iota((rows, cols), 0), iota((rows, cols), 1)
    no_south, no_north = ty == n_ty - 1, ty == 0
    no_east, no_west = tx == n_tx - 1, tx == 0
    first_south = jnp.where(no_south, RY, RY + SUB)
    last_north = jnp.where(no_north, rows, RY + SUB)
    first_east = jnp.where(no_east, RX, RX + REC)
    last_west = jnp.where(no_west, cols, RX + REC)
    inside = ((row < first_south) | (row >= last_north)) & ((col < first_east) | (col >= last_west))

    def spread_wind(which):
        def line(dy):
            w = [around[dy, dx][1][:, REC + which : REC + which + 1] for dx in (0, 1, -1)]
            c = iota((1, cols), 1)
            return jnp.where(c < RX, w[0], jnp.where(c < RX + REC, w[1], w[2]))

        return jnp.where(row < RY, line(0), jnp.where(row < RY + SUB, line(1), line(-1)))

    wind_east, wind_south = spread_wind(0), spread_wind(1)
    field = jnp.where(inside, field, 0.0)
    for _ in range(SUB):
        east, west = pltpu.roll(field, cols - 1, axis=1), pltpu.roll(field, 1, axis=1)
        south, north = pltpu.roll(field, rows - 1, axis=0), pltpu.roll(field, 1, axis=0)
        advect = wind_east * (east - west) + wind_south * (south - north)
        spread = east + west + south + north - 4.0 * field
        field = jnp.where(inside, field - 0.5 * advect + DIFFUSION * spread, 0.0)
    tile = field[0:RY, 0:RX]
    tile_ref[...] = tile
    store = pltpu.make_async_copy(tile_ref, next_ref, sem)
    store.start()

    both = jnp.concatenate([tile, pltpu.roll(tile, RX - 1, axis=1)], axis=1)
    parts = jnp.concatenate(three_terms(both), axis=0)
    records = got_ref[pl.ds(0, tiles, stride=SUB), :]
    line = lax.rem(iota((tiles, 3 * RY), 1), RY).astype(F32)
    lanes = iota((tiles, 128), 1)
    for k in range(CAP):
        at = REC + 4 * k
        cell, frac_row, frac_col = [records[:, at + v : at + v + 1] for v in range(3)]
        cell = jnp.broadcast_to(cell, (tiles, 128))
        row_k = jnp.floor((cell + 0.5) * (1.0 / SPAN))
        col_k = (cell - SPAN * row_k).astype(jnp.int32)
        row_k = jnp.concatenate([row_k, row_k[:, 0 : 3 * RY - 128]], axis=1)
        upper, lower = [
            jnp.dot(
                jnp.where(line == row_k + d, 1.0, 0.0).astype(BF16), parts, preferred_element_type=F32
            )
            for d in (0.0, 1.0)
        ]
        far = lanes < col_k
        spot = (lanes + col_k) & 127
        upper, lower = [
            [
                jnp.where(far, value[:, at + 128 : at + 256], value[:, at : at + 128])
                for at in (0, RX)
            ]
            for value in (upper, lower)
        ]
        rows = [(1.0 - frac_row) * upper[i] + frac_row * lower[i] for i in range(2)]
        steps = [lower[i] - upper[i] for i in range(2)]
        for p, (left, right) in enumerate((rows, steps)):
            value = (1.0 - frac_col) * left + frac_col * right
            reply_ref[pl.ds(2 * k + p, tiles, stride=2 * CAP), :] = jnp.take_along_axis(
                value, spot, axis=1
            )
    store.wait()


def collect_kernel(slot_ref, got_ref, phase_ref, slope_ref, phase_rows, slope_rows, sems):
    records = phase_rows.shape[0]
    part = records // PARTS
    stores = []
    for p in range(PARTS):

        def step(n, carry):
            slot = slot_ref[0, n]
            phase_rows[pl.ds(n, 1), :] = got_ref[pl.ds(slot, 1), :]
            slope_rows[pl.ds(n, 1), :] = got_ref[pl.ds(slot + 1, 1), :]
            return carry

        lax.fori_loop(p * part, (p + 1) * part, step, 0, unroll=UNROLL)
        for i, (rows, out) in enumerate(((phase_rows, phase_ref), (slope_rows, slope_ref))):
            here = pl.ds(p * part, part)
            stores.append(pltpu.make_async_copy(rows.at[here], out.at[here], sems.at[2 * p + i]))
            stores[-1].start()
    for store in stores:
        store.wait()


def local(screen, wind_table, wind_index, tile_id, cell_index, fractions):
    n_ty, n_tx = lax.axis_size("ty"), lax.axis_size("tx")
    tiles = n_ty * n_tx
    groups, width = tile_id.shape[2], tile_id.shape[3]
    records = groups * width

    def shaped(*shape, dtype=F32):
        return jax.ShapeDtypeStruct(shape, dtype)

    send, edges, slots = pl.pallas_call(
        lambda *refs: request_kernel(n_tx, *refs),
        out_shape=(
            shaped(tiles * SUB, 128),
            shaped(2 * SUB, RX),
            pltpu.SMEM((1, records), jnp.int32),
        ),
        in_specs=[SMEM, VMEM] + [HBM] * 4,
        out_specs=(VMEM, VMEM, SMEM),
        scratch_shapes=[
            pltpu.VMEM((1, records), jnp.int32),
            pltpu.SemaphoreType.DMA,
            pltpu.VMEM((RY, RX), F32),
            pltpu.VMEM(wind_table.shape, F32),
            pltpu.VMEM((groups, width), jnp.int32),
            pltpu.VMEM((2, groups, width), F32),
            pltpu.SemaphoreType.DMA((4,)),
        ],
        compiler_params=PARAMS,
        name="make_requests",
    )(
        wind_index,
        tile_id.reshape(groups, 1, width),
        *[
            pltpu.with_memory_space_constraint(x, pltpu.HBM)
            for x in (
                screen,
                wind_table,
                cell_index.reshape(groups, width),
                fractions.reshape(2, groups, width),
            )
        ],
    )

    def exchange(x):
        return lax.all_to_all(x, ("ty", "tx"), split_axis=0, concat_axis=0, tiled=True)

    got = exchange(send)
    north = lax.ppermute(edges, "ty", [(i, (i + 1) % n_ty) for i in range(n_ty)])
    south = lax.ppermute(edges, "ty", [((i + 1) % n_ty, i) for i in range(n_ty)])
    screen_next, reply = pl.pallas_call(
        lambda *refs: sample_kernel(n_ty, n_tx, *refs),
        out_shape=(shaped(RY, RX), shaped(tiles * 2 * CAP, 128)),
        in_specs=[VMEM] * 4,
        out_specs=(HBM, VMEM),
        scratch_shapes=[
            pltpu.VMEM((128, 128), F32),
            pltpu.VMEM((RY, RX), F32),
            pltpu.SemaphoreType.DMA,
        ],
        compiler_params=PARAMS,
        name="step_and_sample",
    )(screen, south, north, got)
    returned = exchange(reply)
    phases, slopes = pl.pallas_call(
        collect_kernel,
        out_shape=(shaped(records, P_SIZE),) * 2,
        in_specs=[SMEM, VMEM],
        out_specs=(HBM,) * 2,
        scratch_shapes=[
            pltpu.VMEM((records, P_SIZE), F32),
            pltpu.VMEM((records, P_SIZE), F32),
            pltpu.SemaphoreType.DMA((2 * PARTS,)),
        ],
        compiler_params=PARAMS,
        name="collect",
    )(slots, returned)
    out_shape = (1, 1, groups, width, P_SIZE)
    return screen_next, phases.reshape(out_shape), slopes.reshape(out_shape)


def solution(mesh):
    in_specs = (
        P("ty", "tx"),
        P(),
        P("ty", "tx"),
        P("ty", "tx", None, None, None),
        P("ty", "tx", None, None),
        P(None, "ty", "tx", None, None),
    )
    out_specs = (P("ty", "tx"), P("ty", "tx", None, None, None), P("ty", "tx", None, None, None))
    return jax.shard_map(local, mesh=mesh, in_specs=in_specs, out_specs=out_specs, check_vma=False)
```

```python
import jax
import jax.numpy as jnp
from jax import lax
from jax.experimental import pallas as pl
from jax.experimental.pallas import tpu as pltpu
from jax.sharding import PartitionSpec as P

RY = 64
RX = 256
P_SIZE = 128
SPAN = RX - P_SIZE - 1
SUB = 4
CAP = 4
DIFFUSION = 0.2
PARTS = 2
UNROLL = 32

REC = 64
F32 = jnp.float32
BF16 = jnp.bfloat16
VMEM = pl.BlockSpec(memory_space=pltpu.VMEM)
SMEM = pl.BlockSpec(memory_space=pltpu.SMEM)
HBM = pl.BlockSpec(memory_space=pltpu.HBM)
PARAMS = pltpu.CompilerParams(vmem_limit_bytes=8 << 20)


def iota(shape, dim):
    return lax.broadcasted_iota(jnp.int32, shape, dim)


def three_terms(x):
    high = x.astype(BF16)
    rest = x - high.astype(F32)
    middle = rest.astype(BF16)
    low = (rest - middle.astype(F32)).astype(BF16)
    return high, middle, low


def request_kernel(n_tx, index_ref, tile_ref, *refs):
    sources, refs = refs[:4], refs[4:]
    (send_ref, edge_ref, slot_out), refs = refs[:3], refs[3:]
    (slot_ref, slot_sem), refs = refs[:2], refs[2:]
    copies = [pltpu.make_async_copy(sources[i], refs[i], refs[4].at[i]) for i in range(4)]
    for copy in copies:
        copy.start()
    screen_ref, table_ref, cell_ref, frac_ref = refs[:4]
    tx = lax.axis_index("tx")
    groups, width = tile_ref.shape[0], tile_ref.shape[2]
    records = groups * width
    tiles = send_ref.shape[0] // SUB
    before = (iota((records, records), 0) < iota((records, records), 1)).astype(F32).astype(BF16)

    def flat(rows):
        return jnp.concatenate(rows, axis=1)

    tile = flat([tile_ref[s] for s in range(groups)])
    names = jnp.where(iota((tiles, records), 0) == tile, 1.0, 0.0)
    earlier = jnp.dot(names.astype(BF16), before, preferred_element_type=F32)
    rank = jnp.sum(names * earlier, axis=0, keepdims=True)
    slot_ref[...] = tile * (2 * CAP) + 2 * rank.astype(jnp.int32)
    slots = pltpu.make_async_copy(slot_ref, slot_out, slot_sem)
    slots.start()

    picks = jnp.concatenate(
        [jnp.where(earlier == k, names, 0.0).astype(BF16) for k in range(CAP)], axis=0
    )
    for copy in copies[2:]:
        copy.wait()
    cell = flat([cell_ref[s : s + 1, :] for s in range(groups)]).astype(F32)
    frac_row = flat([frac_ref[0, s : s + 1, :] for s in range(groups)])
    frac_col = flat([frac_ref[1, s : s + 1, :] for s in range(groups)])
    line = iota((128, records), 0)
    values = jnp.where(
        line == REC,
        cell,
        jnp.where(line == REC + 1, frac_row, jnp.where(line == REC + 2, frac_col, 0.0)),
    )
    found = sum(
        lax.dot_general(picks, part, (((1,), (1,)), ((), ())), preferred_element_type=F32)
        for part in three_terms(values)
    )
    requests = found[0:tiles]
    for k in range(1, CAP):
        requests = requests + pltpu.roll(found[k * tiles : (k + 1) * tiles], 4 * k, axis=1)

    for copy in copies[:2]:
        copy.wait()
    edge_ref[...] = jnp.where(
        iota((2 * SUB, RX), 0) < SUB, screen_ref[0 : 2 * SUB, :], screen_ref[RY - 2 * SUB : RY, :]
    )
    chosen = jnp.where(iota((2, table_ref.shape[1]), 1) == index_ref[0, 0], table_ref[...], 0.0)
    wind = jnp.sum(chosen, axis=1, keepdims=True)
    lane = iota((1, 128), 1)
    winds = jnp.where(lane == REC, wind[0:1], jnp.where(lane == REC + 1, wind[1:2], 0.0))

    blank = jnp.zeros((128 - RY, 128), F32)
    west_cols = jnp.concatenate([screen_ref[:, 0:128], blank], axis=0).T
    east_cols = jnp.concatenate([screen_ref[:, RX - 128 : RX], blank], axis=0).T
    to_east = lax.rem(iota((tiles, 128), 0), n_tx) == tx + 1
    for c in range(SUB):
        row = jnp.where(
            to_east, east_cols[128 - SUB + c : 129 - SUB + c, :], west_cols[c : c + 1, :]
        )
        if c == 0:
            row = row + requests
        if c == 1:
            row = row + winds
        send_ref[pl.ds(c, tiles, stride=SUB), :] = row
    slots.wait()


def sample_kernel(
    n_ty, n_tx, screen_ref, inner_ref, outer_ref, got_ref, next_ref, reply_ref, edge_ref, tile_ref, sem
):
    ty, tx = lax.axis_index("ty"), lax.axis_index("tx")
    tiles = n_ty * n_tx

    def chunk(dy, dx):
        y = jnp.clip(ty + dy, 0, n_ty - 1)
        x = jnp.clip(tx + dx, 0, n_tx - 1)
        return [got_ref[pl.ds((y * n_tx + x) * SUB + c, 1), :] for c in range(SUB)]

    around = {(dy, dx): chunk(dy, dx) for dy in (-1, 0, 1) for dx in (-1, 0, 1)}

    lane = iota((1, 128), 1)
    edge_ref[...] = jnp.zeros((128, 128), F32)
    for dx, start in ((1, 0), (-1, 128 - SUB)):
        for c in range(SUB):
            below = pltpu.roll(around[1, dx][c], RY, axis=1)
            above = pltpu.roll(around[-1, dx][c], 2 * SUB, axis=1)
            edge_ref[start + c : start + c + 1, :] = jnp.where(
                lane < RY, around[0, dx][c], jnp.where(lane < RY + SUB, below, above)
            )
    sides = edge_ref[...].T[0 : RY + 2 * SUB]

    rows, cols = RY + 2 * SUB, RX + 128
    even = lax.rem(ty, 2) == 0
    ends = jnp.where((iota((2 * SUB, RX), 0) < SUB) == even, inner_ref[...], outer_ref[...])
    field = jnp.concatenate(
        [jnp.concatenate([screen_ref[...], ends], axis=0), sides], axis=1
    )
    row, col = iota((rows, cols), 0), iota((rows, cols), 1)
    no_south, no_north = ty == n_ty - 1, ty == 0
    no_east, no_west = tx == n_tx - 1, tx == 0
    first_south = jnp.where(no_south, RY, RY + SUB)
    last_north = jnp.where(no_north, rows, RY + SUB)
    first_east = jnp.where(no_east, RX, RX + REC)
    last_west = jnp.where(no_west, cols, RX + REC)
    inside = ((row < first_south) | (row >= last_north)) & ((col < first_east) | (col >= last_west))

    def spread_wind(which):
        def line(dy):
            w = [around[dy, dx][1][:, REC + which : REC + which + 1] for dx in (0, 1, -1)]
            c = iota((1, cols), 1)
            return jnp.where(c < RX, w[0], jnp.where(c < RX + REC, w[1], w[2]))

        return jnp.where(row < RY, line(0), jnp.where(row < RY + SUB, line(1), line(-1)))

    wind_east, wind_south = spread_wind(0), spread_wind(1)
    field = jnp.where(inside, field, 0.0)
    for _ in range(SUB):
        east, west = pltpu.roll(field, cols - 1, axis=1), pltpu.roll(field, 1, axis=1)
        south, north = pltpu.roll(field, rows - 1, axis=0), pltpu.roll(field, 1, axis=0)
        advect = wind_east * (east - west) + wind_south * (south - north)
        spread = east + west + south + north - 4.0 * field
        field = jnp.where(inside, field - 0.5 * advect + DIFFUSION * spread, 0.0)
    tile = field[0:RY, 0:RX]
    tile_ref[...] = tile
    store = pltpu.make_async_copy(tile_ref, next_ref, sem)
    store.start()

    both = jnp.concatenate([tile, pltpu.roll(tile, RX - 1, axis=1)], axis=1)
    parts = jnp.concatenate(three_terms(both), axis=0)
    records = got_ref[pl.ds(0, tiles, stride=SUB), :]
    line = lax.rem(iota((tiles, 3 * RY), 1), RY).astype(F32)
    lanes = iota((tiles, 128), 1)
    for k in range(CAP):
        at = REC + 4 * k
        cell, frac_row, frac_col = [records[:, at + v : at + v + 1] for v in range(3)]
        cell = jnp.broadcast_to(cell, (tiles, 128))
        row_k = jnp.floor((cell + 0.5) * (1.0 / SPAN))
        col_k = (cell - SPAN * row_k).astype(jnp.int32)
        row_k = jnp.concatenate([row_k, row_k[:, 0 : 3 * RY - 128]], axis=1)
        upper, lower = [
            jnp.dot(
                jnp.where(line == row_k + d, 1.0, 0.0).astype(BF16), parts, preferred_element_type=F32
            )
            for d in (0.0, 1.0)
        ]
        far = lanes < col_k
        spot = (lanes + col_k) & 127
        upper, lower = [
            [
                jnp.where(far, value[:, at + 128 : at + 256], value[:, at : at + 128])
                for at in (0, RX)
            ]
            for value in (upper, lower)
        ]
        rows = [(1.0 - frac_row) * upper[i] + frac_row * lower[i] for i in range(2)]
        steps = [lower[i] - upper[i] for i in range(2)]
        for p, (left, right) in enumerate((rows, steps)):
            value = (1.0 - frac_col) * left + frac_col * right
            reply_ref[pl.ds(2 * k + p, tiles, stride=2 * CAP), :] = jnp.take_along_axis(
                value, spot, axis=1
            )
    store.wait()


def collect_kernel(slot_ref, got_ref, phase_ref, slope_ref, phase_rows, slope_rows, sems):
    records = phase_rows.shape[0]
    part = records // PARTS
    stores = []
    for p in range(PARTS):

        def step(n, carry):
            slot = slot_ref[0, n]
            phase_rows[pl.ds(n, 1), :] = got_ref[pl.ds(slot, 1), :]
            slope_rows[pl.ds(n, 1), :] = got_ref[pl.ds(slot + 1, 1), :]
            return carry

        lax.fori_loop(p * part, (p + 1) * part, step, 0, unroll=UNROLL)
        for i, (rows, out) in enumerate(((phase_rows, phase_ref), (slope_rows, slope_ref))):
            here = pl.ds(p * part, part)
            stores.append(pltpu.make_async_copy(rows.at[here], out.at[here], sems.at[2 * p + i]))
            stores[-1].start()
    for store in stores:
        store.wait()


def local(screen, wind_table, wind_index, tile_id, cell_index, fractions):
    n_ty, n_tx = lax.axis_size("ty"), lax.axis_size("tx")
    tiles = n_ty * n_tx
    groups, width = tile_id.shape[2], tile_id.shape[3]
    records = groups * width

    def shaped(*shape, dtype=F32):
        return jax.ShapeDtypeStruct(shape, dtype)

    send, edges, slots = pl.pallas_call(
        lambda *refs: request_kernel(n_tx, *refs),
        out_shape=(
            shaped(tiles * SUB, 128),
            shaped(2 * SUB, RX),
            pltpu.SMEM((1, records), jnp.int32),
        ),
        in_specs=[SMEM, VMEM] + [HBM] * 4,
        out_specs=(VMEM, VMEM, SMEM),
        scratch_shapes=[
            pltpu.VMEM((1, records), jnp.int32),
            pltpu.SemaphoreType.DMA,
            pltpu.VMEM((RY, RX), F32),
            pltpu.VMEM(wind_table.shape, F32),
            pltpu.VMEM((groups, width), jnp.int32),
            pltpu.VMEM((2, groups, width), F32),
            pltpu.SemaphoreType.DMA((4,)),
        ],
        compiler_params=PARAMS,
        name="make_requests",
    )(
        wind_index,
        tile_id.reshape(groups, 1, width),
        *[
            pltpu.with_memory_space_constraint(x, pltpu.HBM)
            for x in (
                screen,
                wind_table,
                cell_index.reshape(groups, width),
                fractions.reshape(2, groups, width),
            )
        ],
    )

    def exchange(x):
        return lax.all_to_all(x, ("ty", "tx"), split_axis=0, concat_axis=0, tiled=True)

    got = exchange(send)
    def swap(first):
        pairs = []
        for y in range(n_ty):
            other = y + 1 if (y - first) % 2 == 0 else y - 1
            for x in range(n_tx):
                if 0 <= other < n_ty:
                    pairs.append((y * n_tx + x, other * n_tx + x))
                else:
                    pairs.append((y * n_tx + x, y * n_tx + (x ^ 1)))
        return lax.ppermute(edges, ("ty", "tx"), pairs)

    inner, outer = swap(0), swap(1)
    screen_next, reply = pl.pallas_call(
        lambda *refs: sample_kernel(n_ty, n_tx, *refs),
        out_shape=(shaped(RY, RX), shaped(tiles * 2 * CAP, 128)),
        in_specs=[VMEM] * 4,
        out_specs=(HBM, VMEM),
        scratch_shapes=[
            pltpu.VMEM((128, 128), F32),
            pltpu.VMEM((RY, RX), F32),
            pltpu.SemaphoreType.DMA,
        ],
        compiler_params=PARAMS,
        name="step_and_sample",
    )(screen, inner, outer, got)
    returned = exchange(reply)
    phases, slopes = pl.pallas_call(
        collect_kernel,
        out_shape=(shaped(records, P_SIZE),) * 2,
        in_specs=[SMEM, VMEM],
        out_specs=(HBM,) * 2,
        scratch_shapes=[
            pltpu.VMEM((records, P_SIZE), F32),
            pltpu.VMEM((records, P_SIZE), F32),
            pltpu.SemaphoreType.DMA((2 * PARTS,)),
        ],
        compiler_params=PARAMS,
        name="collect",
    )(slots, returned)
    out_shape = (1, 1, groups, width, P_SIZE)
    return screen_next, phases.reshape(out_shape), slopes.reshape(out_shape)


def solution(mesh):
    in_specs = (
        P("ty", "tx"),
        P(),
        P("ty", "tx"),
        P("ty", "tx", None, None, None),
        P("ty", "tx", None, None),
        P(None, "ty", "tx", None, None),
    )
    out_specs = (P("ty", "tx"), P("ty", "tx", None, None, None), P("ty", "tx", None, None, None))
    return jax.shard_map(local, mesh=mesh, in_specs=in_specs, out_specs=out_specs, check_vma=False)
```

```python
import jax
import jax.numpy as jnp
from jax import lax
from jax.experimental import pallas as pl
from jax.experimental.pallas import tpu as pltpu
from jax.sharding import PartitionSpec as P

RY = 64
RX = 256
P_SIZE = 128
SPAN = RX - P_SIZE - 1
SUB = 4
CAP = 4
DIFFUSION = 0.2
PARTS = 2
UNROLL = 32

REC = 64
F32 = jnp.float32
BF16 = jnp.bfloat16
VMEM = pl.BlockSpec(memory_space=pltpu.VMEM)
SMEM = pl.BlockSpec(memory_space=pltpu.SMEM)
HBM = pl.BlockSpec(memory_space=pltpu.HBM)
PARAMS = pltpu.CompilerParams(vmem_limit_bytes=8 << 20)


def iota(shape, dim):
    return lax.broadcasted_iota(jnp.int32, shape, dim)


def three_terms(x):
    high = x.astype(BF16)
    rest = x - high.astype(F32)
    middle = rest.astype(BF16)
    low = (rest - middle.astype(F32)).astype(BF16)
    return high, middle, low


def request_kernel(n_tx, index_ref, tile_ref, *refs):
    sources, refs = refs[:4], refs[4:]
    (send_ref, edge_ref, slot_out), refs = refs[:3], refs[3:]
    (slot_ref, slot_sem), refs = refs[:2], refs[2:]
    copies = [pltpu.make_async_copy(sources[i], refs[i], refs[4].at[i]) for i in range(4)]
    for copy in copies:
        copy.start()
    cell_ref, frac_ref, table_ref, screen_ref = refs[:4]
    tx = lax.axis_index("tx")
    groups, width = tile_ref.shape[0], tile_ref.shape[2]
    records = groups * width
    tiles = send_ref.shape[0] // SUB
    before = (iota((records, records), 0) < iota((records, records), 1)).astype(F32).astype(BF16)

    def flat(rows):
        return jnp.concatenate(rows, axis=1)

    tile = flat([tile_ref[s] for s in range(groups)])
    names = jnp.where(iota((tiles, records), 0) == tile, 1.0, 0.0)
    earlier = jnp.dot(names.astype(BF16), before, preferred_element_type=F32)
    rank = jnp.sum(names * earlier, axis=0, keepdims=True)
    slot_ref[...] = tile * (2 * CAP) + 2 * rank.astype(jnp.int32)
    slots = pltpu.make_async_copy(slot_ref, slot_out, slot_sem)
    slots.start()

    picks = jnp.concatenate(
        [jnp.where(earlier == k, names, 0.0).astype(BF16) for k in range(CAP)], axis=0
    )
    for copy in copies[:2]:
        copy.wait()
    cell = flat([cell_ref[s : s + 1, :] for s in range(groups)]).astype(F32)
    frac_row = flat([frac_ref[0, s : s + 1, :] for s in range(groups)])
    frac_col = flat([frac_ref[1, s : s + 1, :] for s in range(groups)])
    line = iota((128, records), 0)
    values = jnp.where(
        line == REC,
        cell,
        jnp.where(line == REC + 1, frac_row, jnp.where(line == REC + 2, frac_col, 0.0)),
    )
    found = sum(
        lax.dot_general(picks, part, (((1,), (1,)), ((), ())), preferred_element_type=F32)
        for part in three_terms(values)
    )
    requests = found[0:tiles]
    for k in range(1, CAP):
        requests = requests + pltpu.roll(found[k * tiles : (k + 1) * tiles], 4 * k, axis=1)

    for copy in copies[2:]:
        copy.wait()
    edge_ref[...] = jnp.where(
        iota((2 * SUB, RX), 0) < SUB, screen_ref[0 : 2 * SUB, :], screen_ref[RY - 2 * SUB : RY, :]
    )
    chosen = jnp.where(iota((2, table_ref.shape[1]), 1) == index_ref[0, 0], table_ref[...], 0.0)
    wind = jnp.sum(chosen, axis=1, keepdims=True)
    lane = iota((1, 128), 1)
    winds = jnp.where(lane == REC, wind[0:1], jnp.where(lane == REC + 1, wind[1:2], 0.0))

    blank = jnp.zeros((128 - RY, 128), F32)
    west_cols = jnp.concatenate([screen_ref[:, 0:128], blank], axis=0).T
    east_cols = jnp.concatenate([screen_ref[:, RX - 128 : RX], blank], axis=0).T
    to_east = lax.rem(iota((tiles, 128), 0), n_tx) == tx + 1
    for c in range(SUB):
        row = jnp.where(
            to_east, east_cols[128 - SUB + c : 129 - SUB + c, :], west_cols[c : c + 1, :]
        )
        if c == 0:
            row = row + requests
        if c == 1:
            row = row + winds
        send_ref[pl.ds(c, tiles, stride=SUB), :] = row
    slots.wait()


def sample_kernel(
    n_ty, n_tx, screen_ref, inner_ref, outer_ref, cross_ref, got_ref, next_ref, reply_ref, edge_ref, tile_ref, sem
):
    ty, tx = lax.axis_index("ty"), lax.axis_index("tx")
    tiles = n_ty * n_tx

    def chunk(dy, dx):
        y = jnp.clip(ty + dy, 0, n_ty - 1)
        x = jnp.clip(tx + dx, 0, n_tx - 1)
        return [got_ref[pl.ds((y * n_tx + x) * SUB + c, 1), :] for c in range(SUB)]

    around = {(dy, dx): chunk(dy, dx) for dy in (-1, 0, 1) for dx in (-1, 0, 1)}

    lane = iota((1, 128), 1)
    edge_ref[...] = jnp.zeros((128, 128), F32)
    for dx, start in ((1, 0), (-1, 128 - SUB)):
        for c in range(SUB):
            below = pltpu.roll(around[1, dx][c], RY, axis=1)
            above = pltpu.roll(around[-1, dx][c], 2 * SUB, axis=1)
            edge_ref[start + c : start + c + 1, :] = jnp.where(
                lane < RY, around[0, dx][c], jnp.where(lane < RY + SUB, below, above)
            )
    sides = edge_ref[...].T[0 : RY + 2 * SUB]

    rows, cols = RY + 2 * SUB, RX + 128
    even = lax.rem(ty, 2) == 0
    far_pair = lax.rem((ty + 1) // 2, 2) == 0
    outer = jnp.where(far_pair, cross_ref[...], outer_ref[...])
    ends = jnp.where((iota((2 * SUB, RX), 0) < SUB) == even, inner_ref[...], outer)
    field = jnp.concatenate(
        [jnp.concatenate([screen_ref[...], ends], axis=0), sides], axis=1
    )
    row, col = iota((rows, cols), 0), iota((rows, cols), 1)
    no_south, no_north = ty == n_ty - 1, ty == 0
    no_east, no_west = tx == n_tx - 1, tx == 0
    first_south = jnp.where(no_south, RY, RY + SUB)
    last_north = jnp.where(no_north, rows, RY + SUB)
    first_east = jnp.where(no_east, RX, RX + REC)
    last_west = jnp.where(no_west, cols, RX + REC)
    inside = ((row < first_south) | (row >= last_north)) & ((col < first_east) | (col >= last_west))

    def spread_wind(which):
        def line(dy):
            w = [around[dy, dx][1][:, REC + which : REC + which + 1] for dx in (0, 1, -1)]
            c = iota((1, cols), 1)
            return jnp.where(c < RX, w[0], jnp.where(c < RX + REC, w[1], w[2]))

        return jnp.where(row < RY, line(0), jnp.where(row < RY + SUB, line(1), line(-1)))

    wind_east, wind_south = spread_wind(0), spread_wind(1)
    field = jnp.where(inside, field, 0.0)
    for _ in range(SUB):
        east, west = pltpu.roll(field, cols - 1, axis=1), pltpu.roll(field, 1, axis=1)
        south, north = pltpu.roll(field, rows - 1, axis=0), pltpu.roll(field, 1, axis=0)
        advect = wind_east * (east - west) + wind_south * (south - north)
        spread = east + west + south + north - 4.0 * field
        field = jnp.where(inside, field - 0.5 * advect + DIFFUSION * spread, 0.0)
    tile = field[0:RY, 0:RX]
    tile_ref[...] = tile
    store = pltpu.make_async_copy(tile_ref, next_ref, sem)
    store.start()

    both = jnp.concatenate([tile, pltpu.roll(tile, RX - 1, axis=1)], axis=1)
    parts = jnp.concatenate(three_terms(both), axis=0)
    records = got_ref[pl.ds(0, tiles, stride=SUB), :]
    line = lax.rem(iota((tiles, 3 * RY), 1), RY).astype(F32)
    lanes = iota((tiles, 128), 1)
    for k in range(CAP):
        at = REC + 4 * k
        cell, frac_row, frac_col = [records[:, at + v : at + v + 1] for v in range(3)]
        cell = jnp.broadcast_to(cell, (tiles, 128))
        row_k = jnp.floor((cell + 0.5) * (1.0 / SPAN))
        col_k = (cell - SPAN * row_k).astype(jnp.int32)
        row_k = jnp.concatenate([row_k, row_k[:, 0 : 3 * RY - 128]], axis=1)
        upper, lower = [
            jnp.dot(
                jnp.where(line == row_k + d, 1.0, 0.0).astype(BF16), parts, preferred_element_type=F32
            )
            for d in (0.0, 1.0)
        ]
        far = lanes < col_k
        spot = (lanes + col_k) & 127
        upper, lower = [
            [
                jnp.where(far, value[:, at + 128 : at + 256], value[:, at : at + 128])
                for at in (0, RX)
            ]
            for value in (upper, lower)
        ]
        rows = [(1.0 - frac_row) * upper[i] + frac_row * lower[i] for i in range(2)]
        steps = [lower[i] - upper[i] for i in range(2)]
        for p, (left, right) in enumerate((rows, steps)):
            value = (1.0 - frac_col) * left + frac_col * right
            reply_ref[pl.ds(2 * k + p, tiles, stride=2 * CAP), :] = jnp.take_along_axis(
                value, spot, axis=1
            )
    store.wait()


def collect_kernel(slot_ref, got_ref, phase_ref, slope_ref, phase_rows, slope_rows, sems):
    records = phase_rows.shape[0]
    part = records // PARTS
    stores = []
    for p in range(PARTS):

        def step(n, carry):
            slot = slot_ref[0, n]
            phase_rows[pl.ds(n, 1), :] = got_ref[pl.ds(slot, 1), :]
            slope_rows[pl.ds(n, 1), :] = got_ref[pl.ds(slot + 1, 1), :]
            return carry

        lax.fori_loop(p * part, (p + 1) * part, step, 0, unroll=UNROLL)
        for i, (rows, out) in enumerate(((phase_rows, phase_ref), (slope_rows, slope_ref))):
            here = pl.ds(p * part, part)
            stores.append(pltpu.make_async_copy(rows.at[here], out.at[here], sems.at[2 * p + i]))
            stores[-1].start()
    for store in stores:
        store.wait()


def local(screen, wind_table, wind_index, tile_id, cell_index, fractions):
    n_ty, n_tx = lax.axis_size("ty"), lax.axis_size("tx")
    tiles = n_ty * n_tx
    groups, width = tile_id.shape[2], tile_id.shape[3]
    records = groups * width

    def shaped(*shape, dtype=F32):
        return jax.ShapeDtypeStruct(shape, dtype)

    send, edges, slots = pl.pallas_call(
        lambda *refs: request_kernel(n_tx, *refs),
        out_shape=(
            shaped(tiles * SUB, 128),
            shaped(2 * SUB, RX),
            pltpu.SMEM((1, records), jnp.int32),
        ),
        in_specs=[SMEM, VMEM] + [HBM] * 4,
        out_specs=(VMEM, VMEM, SMEM),
        scratch_shapes=[
            pltpu.VMEM((1, records), jnp.int32),
            pltpu.SemaphoreType.DMA,
            pltpu.VMEM((groups, width), jnp.int32),
            pltpu.VMEM((2, groups, width), F32),
            pltpu.VMEM(wind_table.shape, F32),
            pltpu.VMEM((RY, RX), F32),
            pltpu.SemaphoreType.DMA((4,)),
        ],
        compiler_params=PARAMS,
        name="make_requests",
    )(
        wind_index,
        tile_id.reshape(groups, 1, width),
        *[
            pltpu.with_memory_space_constraint(x, pltpu.HBM)
            for x in (
                cell_index.reshape(groups, width),
                fractions.reshape(2, groups, width),
                wind_table,
                screen,
            )
        ],
    )

    def exchange(x):
        return lax.all_to_all(x, ("ty", "tx"), split_axis=0, concat_axis=0, tiled=True)

    got = exchange(send)
    def swap(firsts):
        rows = {i: i + 1 for i in firsts if i + 1 < n_ty}
        rows.update({j: i for i, j in rows.items()})
        pairs = [
            (y * n_tx + x, rows[y] * n_tx + x if y in rows else y * n_tx + (x ^ 1))
            for y in range(n_ty)
            for x in range(n_tx)
        ]
        return lax.ppermute(edges, ("ty", "tx"), pairs)

    inner, outer, cross = [
        swap(range(first, n_ty, step)) for first, step in ((0, 2), (1, 4), (3, 4))
    ]
    screen_next, reply = pl.pallas_call(
        lambda *refs: sample_kernel(n_ty, n_tx, *refs),
        out_shape=(shaped(RY, RX), shaped(tiles * 2 * CAP, 128)),
        in_specs=[VMEM] * 5,
        out_specs=(HBM, VMEM),
        scratch_shapes=[
            pltpu.VMEM((128, 128), F32),
            pltpu.VMEM((RY, RX), F32),
            pltpu.SemaphoreType.DMA,
        ],
        compiler_params=PARAMS,
        name="step_and_sample",
    )(screen, inner, outer, cross, got)
    returned = exchange(reply)
    phases, slopes = pl.pallas_call(
        collect_kernel,
        out_shape=(shaped(records, P_SIZE),) * 2,
        in_specs=[SMEM, VMEM],
        out_specs=(HBM,) * 2,
        scratch_shapes=[
            pltpu.VMEM((records, P_SIZE), F32),
            pltpu.VMEM((records, P_SIZE), F32),
            pltpu.SemaphoreType.DMA((2 * PARTS,)),
        ],
        compiler_params=PARAMS,
        name="collect",
    )(slots, returned)
    out_shape = (1, 1, groups, width, P_SIZE)
    return screen_next, phases.reshape(out_shape), slopes.reshape(out_shape)


def solution(mesh):
    in_specs = (
        P("ty", "tx"),
        P(),
        P("ty", "tx"),
        P("ty", "tx", None, None, None),
        P("ty", "tx", None, None),
        P(None, "ty", "tx", None, None),
    )
    out_specs = (P("ty", "tx"), P("ty", "tx", None, None, None), P("ty", "tx", None, None, None))
    return jax.shard_map(local, mesh=mesh, in_specs=in_specs, out_specs=out_specs, check_vma=False)
```

```python
import jax
import jax.numpy as jnp
from jax import lax
from jax.experimental import pallas as pl
from jax.experimental.pallas import tpu as pltpu
from jax.sharding import PartitionSpec as P

RY = 64
RX = 256
P_SIZE = 128
SPAN = RX - P_SIZE - 1
SUB = 4
CAP = 4
DIFFUSION = 0.2
PARTS = 4
UNROLL = 64

REC = 64
F32 = jnp.float32
BF16 = jnp.bfloat16
VMEM = pl.BlockSpec(memory_space=pltpu.VMEM)
SMEM = pl.BlockSpec(memory_space=pltpu.SMEM)
HBM = pl.BlockSpec(memory_space=pltpu.HBM)
PARAMS = pltpu.CompilerParams(vmem_limit_bytes=8 << 20)


def iota(shape, dim):
    return lax.broadcasted_iota(jnp.int32, shape, dim)


def three_terms(x):
    high = x.astype(BF16)
    rest = x - high.astype(F32)
    middle = rest.astype(BF16)
    low = (rest - middle.astype(F32)).astype(BF16)
    return high, middle, low


def request_kernel(n_tx, index_ref, tile_ref, *refs):
    sources, refs = refs[:4], refs[4:]
    (send_ref, edge_ref, slot_out), refs = refs[:3], refs[3:]
    (slot_ref, slot_sem), refs = refs[:2], refs[2:]
    copies = [pltpu.make_async_copy(sources[i], refs[i], refs[4].at[i]) for i in range(4)]
    for copy in copies:
        copy.start()
    screen_ref, table_ref, cell_ref, frac_ref = refs[:4]
    tx = lax.axis_index("tx")
    groups, width = tile_ref.shape[0], tile_ref.shape[2]
    records = groups * width
    tiles = send_ref.shape[0] // SUB
    before = (iota((records, records), 0) < iota((records, records), 1)).astype(F32).astype(BF16)

    def flat(rows):
        return jnp.concatenate(rows, axis=1)

    tile = flat([tile_ref[s] for s in range(groups)])
    names = jnp.where(iota((tiles, records), 0) == tile, 1.0, 0.0)
    earlier = jnp.dot(names.astype(BF16), before, preferred_element_type=F32)
    rank = jnp.sum(names * earlier, axis=0, keepdims=True)
    slot_ref[...] = tile * (2 * CAP) + 2 * rank.astype(jnp.int32)
    slots = pltpu.make_async_copy(slot_ref, slot_out, slot_sem)
    slots.start()

    picks = jnp.concatenate(
        [jnp.where(earlier == k, names, 0.0).astype(BF16) for k in range(CAP)], axis=0
    )
    for copy in copies[2:]:
        copy.wait()
    cell = flat([cell_ref[s : s + 1, :] for s in range(groups)]).astype(F32)
    frac_row = flat([frac_ref[0, s : s + 1, :] for s in range(groups)])
    frac_col = flat([frac_ref[1, s : s + 1, :] for s in range(groups)])
    line = iota((128, records), 0)
    values = jnp.where(
        line == REC,
        cell,
        jnp.where(line == REC + 1, frac_row, jnp.where(line == REC + 2, frac_col, 0.0)),
    )
    found = sum(
        lax.dot_general(picks, part, (((1,), (1,)), ((), ())), preferred_element_type=F32)
        for part in three_terms(values)
    )
    requests = found[0:tiles]
    for k in range(1, CAP):
        requests = requests + pltpu.roll(found[k * tiles : (k + 1) * tiles], 4 * k, axis=1)

    for copy in copies[:2]:
        copy.wait()
    edge_ref[...] = jnp.where(
        iota((2 * SUB, RX), 0) < SUB, screen_ref[0 : 2 * SUB, :], screen_ref[RY - 2 * SUB : RY, :]
    )
    chosen = jnp.where(iota((2, table_ref.shape[1]), 1) == index_ref[0, 0], table_ref[...], 0.0)
    wind = jnp.sum(chosen, axis=1, keepdims=True)
    lane = iota((1, 128), 1)
    winds = jnp.where(lane == REC, wind[0:1], jnp.where(lane == REC + 1, wind[1:2], 0.0))

    blank = jnp.zeros((128 - RY, 128), F32)
    west_cols = jnp.concatenate([screen_ref[:, 0:128], blank], axis=0).T
    east_cols = jnp.concatenate([screen_ref[:, RX - 128 : RX], blank], axis=0).T
    to_east = lax.rem(iota((tiles, 128), 0), n_tx) == tx + 1
    for c in range(SUB):
        row = jnp.where(
            to_east, east_cols[128 - SUB + c : 129 - SUB + c, :], west_cols[c : c + 1, :]
        )
        if c == 0:
            row = row + requests
        if c == 1:
            row = row + winds
        send_ref[pl.ds(c, tiles, stride=SUB), :] = row
    slots.wait()


def sample_kernel(
    n_ty, n_tx, screen_ref, inner_ref, outer_ref, got_ref, next_ref, reply_ref, edge_ref, tile_ref, sem
):
    ty, tx = lax.axis_index("ty"), lax.axis_index("tx")
    tiles = n_ty * n_tx

    def chunk(dy, dx):
        y = jnp.clip(ty + dy, 0, n_ty - 1)
        x = jnp.clip(tx + dx, 0, n_tx - 1)
        return [got_ref[pl.ds((y * n_tx + x) * SUB + c, 1), :] for c in range(SUB)]

    around = {(dy, dx): chunk(dy, dx) for dy in (-1, 0, 1) for dx in (-1, 0, 1)}

    lane = iota((1, 128), 1)
    edge_ref[...] = jnp.zeros((128, 128), F32)
    for dx, start in ((1, 0), (-1, 128 - SUB)):
        for c in range(SUB):
            below = pltpu.roll(around[1, dx][c], RY, axis=1)
            above = pltpu.roll(around[-1, dx][c], 2 * SUB, axis=1)
            edge_ref[start + c : start + c + 1, :] = jnp.where(
                lane < RY, around[0, dx][c], jnp.where(lane < RY + SUB, below, above)
            )
    sides = edge_ref[...].T[0 : RY + 2 * SUB]

    rows, cols = RY + 2 * SUB, RX + 128
    even = lax.rem(ty, 2) == 0
    ends = jnp.where((iota((2 * SUB, RX), 0) < SUB) == even, inner_ref[...], outer_ref[...])
    field = jnp.concatenate(
        [jnp.concatenate([screen_ref[...], ends], axis=0), sides], axis=1
    )
    row, col = iota((rows, cols), 0), iota((rows, cols), 1)
    no_south, no_north = ty == n_ty - 1, ty == 0
    no_east, no_west = tx == n_tx - 1, tx == 0
    first_south = jnp.where(no_south, RY, RY + SUB)
    last_north = jnp.where(no_north, rows, RY + SUB)
    first_east = jnp.where(no_east, RX, RX + REC)
    last_west = jnp.where(no_west, cols, RX + REC)
    inside = ((row < first_south) | (row >= last_north)) & ((col < first_east) | (col >= last_west))

    def spread_wind(which):
        def line(dy):
            w = [around[dy, dx][1][:, REC + which : REC + which + 1] for dx in (0, 1, -1)]
            c = iota((1, cols), 1)
            return jnp.where(c < RX, w[0], jnp.where(c < RX + REC, w[1], w[2]))

        return jnp.where(row < RY, line(0), jnp.where(row < RY + SUB, line(1), line(-1)))

    wind_east, wind_south = spread_wind(0), spread_wind(1)
    field = jnp.where(inside, field, 0.0)
    for _ in range(SUB):
        east, west = pltpu.roll(field, cols - 1, axis=1), pltpu.roll(field, 1, axis=1)
        south, north = pltpu.roll(field, rows - 1, axis=0), pltpu.roll(field, 1, axis=0)
        advect = wind_east * (east - west) + wind_south * (south - north)
        spread = east + west + south + north - 4.0 * field
        field = jnp.where(inside, field - 0.5 * advect + DIFFUSION * spread, 0.0)
    tile = field[0:RY, 0:RX]
    tile_ref[...] = tile
    store = pltpu.make_async_copy(tile_ref, next_ref, sem)
    store.start()

    both = jnp.concatenate([tile, pltpu.roll(tile, RX - 1, axis=1)], axis=1)
    parts = jnp.concatenate(three_terms(both), axis=0)
    records = got_ref[pl.ds(0, tiles, stride=SUB), :]
    line = lax.rem(iota((tiles, 3 * RY), 1), RY).astype(F32)
    lanes = iota((tiles, 128), 1)
    for k in range(CAP):
        at = REC + 4 * k
        cell, frac_row, frac_col = [records[:, at + v : at + v + 1] for v in range(3)]
        cell = jnp.broadcast_to(cell, (tiles, 128))
        row_k = jnp.floor((cell + 0.5) * (1.0 / SPAN))
        col_k = (cell - SPAN * row_k).astype(jnp.int32)
        row_k = jnp.concatenate([row_k, row_k[:, 0 : 3 * RY - 128]], axis=1)
        picked = jnp.dot(
            jnp.concatenate(
                [jnp.where(line == row_k + d, 1.0, 0.0).astype(BF16) for d in (0.0, 1.0)], axis=0
            ),
            parts,
            preferred_element_type=F32,
        )
        upper, lower = picked[0:tiles], picked[tiles:]
        far = lanes < col_k
        spot = (lanes + col_k) & 127
        upper, lower = [
            [
                jnp.where(far, value[:, at + 128 : at + 256], value[:, at : at + 128])
                for at in (0, RX)
            ]
            for value in (upper, lower)
        ]
        rows = [(1.0 - frac_row) * upper[i] + frac_row * lower[i] for i in range(2)]
        steps = [lower[i] - upper[i] for i in range(2)]
        for p, (left, right) in enumerate((rows, steps)):
            value = (1.0 - frac_col) * left + frac_col * right
            reply_ref[pl.ds(2 * k + p, tiles, stride=2 * CAP), :] = jnp.take_along_axis(
                value, spot, axis=1
            )
    store.wait()


def collect_kernel(slot_ref, got_ref, phase_ref, slope_ref, phase_rows, slope_rows, sems):
    records = phase_rows.shape[0]
    part = records // PARTS
    stores = []
    for p in range(PARTS):

        def step(n, carry):
            slot = slot_ref[0, n]
            phase_rows[pl.ds(n, 1), :] = got_ref[pl.ds(slot, 1), :]
            slope_rows[pl.ds(n, 1), :] = got_ref[pl.ds(slot + 1, 1), :]
            return carry

        lax.fori_loop(p * part, (p + 1) * part, step, 0, unroll=UNROLL)
        for i, (rows, out) in enumerate(((phase_rows, phase_ref), (slope_rows, slope_ref))):
            here = pl.ds(p * part, part)
            stores.append(pltpu.make_async_copy(rows.at[here], out.at[here], sems.at[2 * p + i]))
            stores[-1].start()
    for store in stores:
        store.wait()


def local(screen, wind_table, wind_index, tile_id, cell_index, fractions):
    n_ty, n_tx = lax.axis_size("ty"), lax.axis_size("tx")
    tiles = n_ty * n_tx
    groups, width = tile_id.shape[2], tile_id.shape[3]
    records = groups * width

    def shaped(*shape, dtype=F32):
        return jax.ShapeDtypeStruct(shape, dtype)

    send, edges, slots = pl.pallas_call(
        lambda *refs: request_kernel(n_tx, *refs),
        out_shape=(
            shaped(tiles * SUB, 128),
            shaped(2 * SUB, RX),
            pltpu.SMEM((1, records), jnp.int32),
        ),
        in_specs=[SMEM, VMEM] + [HBM] * 4,
        out_specs=(VMEM, VMEM, SMEM),
        scratch_shapes=[
            pltpu.VMEM((1, records), jnp.int32),
            pltpu.SemaphoreType.DMA,
            pltpu.VMEM((RY, RX), F32),
            pltpu.VMEM(wind_table.shape, F32),
            pltpu.VMEM((groups, width), jnp.int32),
            pltpu.VMEM((2, groups, width), F32),
            pltpu.SemaphoreType.DMA((4,)),
        ],
        compiler_params=PARAMS,
        name="make_requests",
    )(
        wind_index,
        tile_id.reshape(groups, 1, width),
        *[
            pltpu.with_memory_space_constraint(x, pltpu.HBM)
            for x in (
                screen,
                wind_table,
                cell_index.reshape(groups, width),
                fractions.reshape(2, groups, width),
            )
        ],
    )

    def exchange(x):
        return lax.all_to_all(x, ("ty", "tx"), split_axis=0, concat_axis=0, tiled=True)

    got = exchange(send)
    def swap(first):
        pairs = []
        for y in range(n_ty):
            other = y + 1 if (y - first) % 2 == 0 else y - 1
            for x in range(n_tx):
                if 0 <= other < n_ty:
                    pairs.append((y * n_tx + x, other * n_tx + x))
                else:
                    pairs.append((y * n_tx + x, y * n_tx + (x ^ 1)))
        return lax.ppermute(edges, ("ty", "tx"), pairs)

    inner, outer = swap(0), swap(1)
    screen_next, reply = pl.pallas_call(
        lambda *refs: sample_kernel(n_ty, n_tx, *refs),
        out_shape=(shaped(RY, RX), shaped(tiles * 2 * CAP, 128)),
        in_specs=[VMEM] * 4,
        out_specs=(HBM, VMEM),
        scratch_shapes=[
            pltpu.VMEM((128, 128), F32),
            pltpu.VMEM((RY, RX), F32),
            pltpu.SemaphoreType.DMA,
        ],
        compiler_params=PARAMS,
        name="step_and_sample",
    )(screen, inner, outer, got)
    returned = exchange(reply)
    phases, slopes = pl.pallas_call(
        collect_kernel,
        out_shape=(shaped(records, P_SIZE),) * 2,
        in_specs=[SMEM, VMEM],
        out_specs=(HBM,) * 2,
        scratch_shapes=[
            pltpu.VMEM((records, P_SIZE), F32),
            pltpu.VMEM((records, P_SIZE), F32),
            pltpu.SemaphoreType.DMA((2 * PARTS,)),
        ],
        compiler_params=PARAMS,
        name="collect",
    )(slots, returned)
    out_shape = (1, 1, groups, width, P_SIZE)
    return screen_next, phases.reshape(out_shape), slopes.reshape(out_shape)


def solution(mesh):
    in_specs = (
        P("ty", "tx"),
        P(),
        P("ty", "tx"),
        P("ty", "tx", None, None, None),
        P("ty", "tx", None, None),
        P(None, "ty", "tx", None, None),
    )
    out_specs = (P("ty", "tx"), P("ty", "tx", None, None, None), P("ty", "tx", None, None, None))
    return jax.shard_map(local, mesh=mesh, in_specs=in_specs, out_specs=out_specs, check_vma=False)
```
